512 devices in a mesh: section: 16 (over x, z_hi, core), dp: 32 (over y, z_lo).
Axes of the slice: x: 4, y: 4, z: 16 (z_hi: 2, z_lo: 8; z = z_hi * 8 + z_lo), core: 2. Of those that a mesh axis runs over, the one named last changes fastest.
Arguments:
- arriving_activations: bfloat16 [16, 64, 12, 12, 256], P('section', 'dp'), may hold values from -6 to 6
- fresh_images: bfloat16 [3, 64, 12, 12, 256], P(None, 'dp'), may hold values from -6 to 6
- saved_inputs: bfloat16 [4, 16, 64, 12, 12, 256], P(None, 'section', 'dp'), may hold values from -6 to 6
- arriving_gradients: bfloat16 [16, 64, 12, 12, 256], P('section', 'dp'), may hold values from -6 to 6
- fresh_gradients: bfloat16 [3, 64, 12, 12, 256], P(None, 'dp'), may hold values from -6 to 6
- feed_order: int32 [3], replicated, may hold values from 0 to 2, each once
- forward_weight: bfloat16 [16, 2304, 256], P('section'), may hold values from -0.125 to 0.125
- forward_gain: float32 [16, 256], P('section'), may hold values from 0.1 to 1.9
- forward_bias: float32 [16, 256], P('section'), may hold values from -3 to 3
- backward_weight: bfloat16 [16, 2304, 256], P('section'), may hold values from -0.125 to 0.125
- backward_gain: float32 [16, 256], P('section'), may hold values from 0.1 to 1.9
- backward_bias: float32 [16, 256], P('section'), may hold values from -3 to 3
Outputs:
- section_outputs: float32 [4, 16, 64, 12, 12, 256], P(None, 'section', 'dp')
- input_gradients: float32 [4, 16, 64, 12, 12, 256], P(None, 'section', 'dp')
- weight_gradient: float32 [16, 2304, 256], P('section', 'dp')
The draws below stay inside these ranges and needn't reach their ends.
Inputs may be any that keep to these rules, and one draw needn't show every extreme that they name: `feed_order`: each of 0 to 2 appears once.
All inputs are finite; a program needn't handle non-finite values.
Results may differ from the reference program's by a relative error of at most 0.0044.
Values sent between devices are 32-bit elements; how exact they have to be, the bound alone decides.
A program may use at most 64 MiB of HBM per device.

```python
import jax
import jax.numpy as jnp
from jax import lax

C = 256
GROUPS = 32
HH = 12
WW = 12
TICKS = 4
BATCH = 64
N_LAYERS = 16


def levels(rng, extent, split, smallest, high):
    def one(position, blocks):
        steps = jax.random.uniform(jax.random.fold_in(jax.random.fold_in(rng, 6), position), (blocks,), jnp.float32, smallest / len(split), high / len(split))
        return jnp.repeat(jnp.exp(steps), extent[position] // blocks).reshape((-1,) + (1,) * (len(extent) - position - 1))

    loudness = one(*split[0])
    for cut in split[1:]:
        loudness = loudness * one(*cut)
    return loudness


def centred(key, shape, width, reach, shards=(), kind=jnp.bfloat16):
    values = width * jax.random.normal(key, shape, jnp.float32)
    if shards:
        values = values * levels(key, shape, shards, -0.22, 0.18)
    return jnp.clip(values, -reach, reach).astype(kind)


def setup_inputs(seed: int = 0) -> dict:
    keys = jax.random.split(jax.random.key(seed), 13)
    return {
        "arriving_activations": centred(keys[0], (N_LAYERS, BATCH, HH, WW, C), 1.0, 6.0, ((0, 16), (1, 32))),
        "fresh_images": centred(keys[1], (TICKS - 1, BATCH, HH, WW, C), 1.0, 6.0, ((1, 32),)),
        "saved_inputs": centred(keys[2], (TICKS, N_LAYERS, BATCH, HH, WW, C), 1.0, 6.0, ((1, 16), (2, 32))),
        "arriving_gradients": centred(keys[3], (N_LAYERS, BATCH, HH, WW, C), 1.0, 6.0, ((0, 16), (1, 32))),
        "fresh_gradients": centred(keys[4], (TICKS - 1, BATCH, HH, WW, C), 1.0, 6.0, ((1, 32),)),
        "feed_order": jax.random.permutation(keys[5], TICKS - 1).astype(jnp.int32),
        "forward_weight": centred(keys[6], (N_LAYERS, 9 * C, C), (9 * C) ** -0.5, 0.125, ((0, 16),)),
        "forward_gain": jnp.clip(1.0 + 0.18 * jax.random.normal(keys[7], (N_LAYERS, C), jnp.float32), 0.1, 1.9),
        "forward_bias": centred(keys[8], (N_LAYERS, C), 0.5, 3.0, ((0, 16),), jnp.float32),
        "backward_weight": centred(keys[9], (N_LAYERS, 9 * C, C), (9 * C) ** -0.5, 0.125, ((0, 16),)),
        "backward_gain": jnp.clip(1.0 + 0.18 * jax.random.normal(keys[10], (N_LAYERS, C), jnp.float32), 0.1, 1.9),
        "backward_bias": centred(keys[11], (N_LAYERS, C), 0.5, 3.0, ((0, 16),), jnp.float32),
    }


def group_norm_silu(values, gain, bias):
    grouped = values.reshape(values.shape[0], values.shape[1] * values.shape[2], GROUPS, -1)
    average = lax.optimization_barrier(jnp.mean(grouped, axis=(1, 3), keepdims=True))
    spread = lax.optimization_barrier(jnp.mean(jnp.square(grouped - average), axis=(1, 3), keepdims=True))
    normed = ((grouped - average) * lax.rsqrt(spread + 1e-05)).reshape(values.shape)
    scaled = normed * gain + bias
    return scaled * jax.nn.sigmoid(scaled)

def patches(images):
    rows = images.shape[1]
    cols = images.shape[2]
    padded = jnp.pad(images, ((0, 0), (1, 1), (1, 1), (0, 0)))
    shifted = [padded[:, shift_row:shift_row + rows, shift_col:shift_col + cols, :] for shift_row in range(3) for shift_col in range(3)]
    return jnp.concatenate(shifted, axis=-1).reshape(-1, 9 * images.shape[3])

def flipped(weight):
    channels = weight.shape[1]
    return weight.reshape(3, 3, channels, channels)[::-1, ::-1].transpose(0, 1, 3, 2).reshape(9 * channels, channels)

def forward_layer(inputs, weight, gain, bias):
    widened = inputs.astype(jnp.float32)
    hidden = group_norm_silu(widened, gain, bias).astype(jnp.bfloat16)
    convolved = jnp.dot(patches(hidden), weight, preferred_element_type=jnp.float32).reshape(inputs.shape)
    return widened + convolved

def backward_layer(saved, incoming, weight, gain, bias):
    widened = saved.astype(jnp.float32)
    activated, pullback = jax.vjp(lambda values: group_norm_silu(values, gain, bias), widened)
    hidden = activated.astype(jnp.bfloat16)
    narrow = incoming.astype(jnp.bfloat16)
    hidden_grad = jnp.dot(patches(narrow), flipped(weight), preferred_element_type=jnp.float32).reshape(saved.shape)
    through_norm, = pullback(hidden_grad)
    gradient = incoming.astype(jnp.float32) + through_norm
    incoming_rows = narrow.reshape(-1, narrow.shape[3])
    term = lax.dot_general(patches(hidden), incoming_rows, (((0,), (0,)), ((), ())), preferred_element_type=jnp.float32)
    return (gradient, term)

def reference(arriving_activations, fresh_images, saved_inputs, arriving_gradients, fresh_gradients, feed_order, forward_weight, forward_gain, forward_bias, backward_weight, backward_gain, backward_bias):
    act_in = arriving_activations.astype(jnp.float32)
    grad_in = arriving_gradients.astype(jnp.float32)
    emitted = []
    returned = []
    weight_total = jnp.zeros(backward_weight.shape, jnp.float32)
    act_out = act_in
    grad_out = grad_in
    for tick_num in range(TICKS):
        if tick_num > 0:
            index = feed_order[tick_num - 1].astype(jnp.int32)
            chosen = lax.dynamic_index_in_dim(fresh_images, index, 0, keepdims=True).astype(jnp.float32)
            act_in = jnp.concatenate([chosen, act_out[:-1]], axis=0)
            chosen_grad = lax.dynamic_index_in_dim(fresh_gradients, index, 0, keepdims=True).astype(jnp.float32)
            grad_in = jnp.concatenate([chosen_grad, grad_out[:-1]], axis=0)
        act_out = lax.map(lambda packed: forward_layer(*packed), (act_in, forward_weight, forward_gain, forward_bias))
        grad_out, terms = lax.map(lambda packed: backward_layer(*packed), (saved_inputs[tick_num], grad_in, backward_weight, backward_gain, backward_bias))
        weight_total = weight_total + terms
        emitted.append(act_out)
        returned.append(grad_out)
    return (jnp.stack(emitted), jnp.stack(returned), weight_total * (1.0 / BATCH))
```

```python
import jax
import jax.numpy as jnp
from jax import lax
from jax.experimental import pallas as pl
from jax.experimental.pallas import tpu as pltpu
from jax.sharding import PartitionSpec as P

C = 256
TAPS = 9
SIDE = 12
PAD = 16
IMAGES = 2
LINES = IMAGES * SIDE
ROWS = LINES * PAD
PACKED = LINES * SIDE
TICKS = 4
SECTIONS = 16
GROUP = 8
NY = 4
NZ = 8
BLOCK = 72
PARTS = 3
PIECE = BLOCK // PARTS
EPS = 1e-05
COUNT = SIDE * SIDE * GROUP
BATCH = 64
MESH = pl.DeviceIdType.MESH
F32 = jnp.float32
BF16 = jnp.bfloat16


def group_mean(columns):
    lane = lax.broadcasted_iota(jnp.int32, columns.shape, 1)
    for step in (1, 2, 4):
        below = pltpu.roll(columns, step, 1)
        above = pltpu.roll(columns, C - step, 1)
        columns = columns + jnp.where((lane & step) == 0, above, below)
    return columns * (1.0 / COUNT)


def per_image(values):
    return jnp.sum(values.reshape(IMAGES, SIDE * PAD, C), axis=1)


def spread_out(columns):
    return jnp.broadcast_to(columns[:, None, :], (IMAGES, SIDE * PAD, C)).reshape(ROWS, C)


def normed(values, inside):
    average = spread_out(group_mean(per_image(jnp.where(inside, values, 0.0))))
    centred = jnp.where(inside, values - average, 0.0)
    spread = group_mean(per_image(centred * centred))
    scale = lax.rsqrt(spread + EPS)
    return centred * spread_out(scale), scale


def kernel(
    order_ref,
    act_ref,
    fresh_act_ref,
    saved_ref,
    grad_ref,
    fresh_grad_ref,
    fw_ref,
    fgain_ref,
    fbias_ref,
    bw_ref,
    bgain_ref,
    bbias_ref,
    emitted_ref,
    returned_ref,
    wgrad_ref,
    x_buf,
    e_buf,
    xhat_buf,
    slope_buf,
    scale_buf,
    turned_buf,
    bwt_buf,
    hp_buf,
    ep_buf,
    total_buf,
    act_out,
    act_in,
    grad_out,
    grad_in,
    y_in,
    y_sum,
    z_in,
    act_send,
    act_recv,
    grad_send,
    grad_recv,
    y_send,
    y_recv,
    z_send,
    z_recv,
):
    section = lax.axis_index("section")
    shard = lax.axis_index("dp")
    my_y = shard // NZ
    my_z = lax.rem(shard, NZ)

    barrier = pltpu.get_barrier_semaphore()
    for near in (lax.rem(section + 1, SECTIONS), lax.rem(section + SECTIONS - 1, SECTIONS)):
        pl.semaphore_signal(
            barrier, inc=1, device_id={"section": near, "dp": shard}, device_id_type=MESH
        )
    for k in range(1, NY):
        peer = lax.rem(my_y + k, NY) * NZ + my_z
        pl.semaphore_signal(
            barrier, inc=1, device_id={"section": section, "dp": peer}, device_id_type=MESH
        )
    for k in range(1, NZ):
        peer = my_y * NZ + lax.rem(my_z + k, NZ)
        pl.semaphore_signal(
            barrier, inc=1, device_id={"section": section, "dp": peer}, device_id_type=MESH
        )

    place = lax.broadcasted_iota(jnp.int32, (ROWS, C), 0)
    inside = (place & (PAD - 1)) < SIDE
    low_half = lax.broadcasted_iota(jnp.int32, (LINES // 2, 8, C), 1) < 4

    x_buf[...] = jnp.zeros_like(x_buf)
    e_buf[...] = jnp.zeros_like(e_buf)
    hp_buf[...] = jnp.zeros_like(hp_buf)
    ep_buf[...] = jnp.zeros_like(ep_buf)

    def store_shifted(buf, values):
        for kc, moved in enumerate((pltpu.roll(values, 1, 0), values, pltpu.roll(values, ROWS - 1, 0))):
            buf[kc, :, 1 : SIDE + 1] = moved.astype(BF16).reshape(IMAGES, SIDE, PAD, C)

    def columns_of(buf):
        return jnp.concatenate(
            [
                buf[kc, :, kr : kr + SIDE].reshape(ROWS, C)
                for kr in range(3)
                for kc in range(3)
            ],
            axis=1,
        )

    def pack(out, values):
        lines = values.reshape(LINES // 2, 2, PAD, C)
        out[0:LINES] = lines[:, :, 0:8].reshape(LINES, 8, C)
        rest = lines[:, :, 8:16]
        second = pltpu.roll(rest[:, 1].reshape(LINES // 2 * 8, C), 4, 0).reshape(LINES // 2, 8, C)
        out[LINES : LINES + LINES // 2] = jnp.where(low_half, rest[:, 0], second)

    def unpack(buf, source):
        buf[:, 0:8] = source[0:LINES]
        rest = source[LINES : LINES + LINES // 2]
        down = pltpu.roll(rest.reshape(LINES // 2 * 8, C), LINES // 2 * 8 - 4, 0).reshape(
            LINES // 2, 8, C
        )
        both = jnp.where(low_half, rest, 0.0), jnp.where(low_half, down, 0.0)
        buf[:, 8:16] = jnp.stack(both, axis=1).reshape(LINES, 8, C)

    def sender(out, into, send, recv, tick):
        return pltpu.make_async_remote_copy(
            src_ref=out.at[tick],
            dst_ref=into.at[tick],
            send_sem=send.at[tick],
            recv_sem=recv.at[tick],
            device_id={"section": lax.rem(section + 1, SECTIONS), "dp": shard},
            device_id_type=MESH,
        )

    def send_on(*stream):
        @pl.when(section < SECTIONS - 1)
        def _():
            sender(*stream).start()

    def take(buf, fresh_ref, stream, tick):
        @pl.when(section == 0)
        def _():
            buf[:, 0:SIDE] = fresh_ref[order_ref[tick - 1]].astype(F32)

        @pl.when(section > 0)
        def _():
            sender(*stream).wait_recv()
            unpack(buf, stream[1].at[tick - 1])

    act_stream = lambda tick: (act_out, act_in, act_send, act_recv, tick)
    grad_stream = lambda tick: (grad_out, grad_in, grad_send, grad_recv, tick)

    def prepare(tick):
        x_buf[:, 0:SIDE] = saved_ref[tick].astype(F32)
        x_buf[:, SIDE:PAD] = jnp.zeros((LINES, PAD - SIDE, C), F32)
        xhat, scale = normed(x_buf[...].reshape(ROWS, C), inside)
        gain = bgain_ref[...]
        scaled = xhat * gain + bbias_ref[...]
        gate = 1.0 / (1.0 + jnp.exp(-scaled))
        hidden = jnp.where(inside, scaled * gate, 0.0)
        slope = gate * (1.0 + scaled * (1.0 - gate)) * gain
        xhat_buf[tick] = xhat
        slope_buf[tick] = jnp.where(inside, slope, 0.0)
        scale_buf[tick] = scale
        for kc, moved in enumerate((pltpu.roll(hidden, 1, 0), hidden, pltpu.roll(hidden, ROWS - 1, 0))):
            turned_buf[tick, kc * C : (kc + 1) * C] = moved.T.astype(BF16)

    def backward(tick):
        incoming = e_buf[...].reshape(ROWS, C)
        store_shifted(ep_buf, incoming)
        hidden_grad = jnp.dot(columns_of(ep_buf), bwt_buf[...], preferred_element_type=F32)
        through = hidden_grad * slope_buf[tick]
        xhat = xhat_buf[tick]
        level = spread_out(group_mean(per_image(through)))
        tilt = spread_out(group_mean(per_image(through * xhat)))
        result = incoming + spread_out(scale_buf[tick]) * (through - level - xhat * tilt)
        returned_ref[tick] = result.reshape(LINES, PAD, C)[:, 0:SIDE]
        return result

    def weight_terms(tick):
        for kr in range(3):
            shifted = ep_buf[1, :, 2 - kr : 2 - kr + SIDE].reshape(ROWS, C)
            term = jnp.dot(turned_buf[tick], shifted, preferred_element_type=F32)
            rows = pl.ds(kr * 3 * C, 3 * C)
            if tick == 0:
                total_buf[rows] = term
            else:
                total_buf[rows] += term

    def forward(tick):
        values = x_buf[...].reshape(ROWS, C)
        xhat, _ = normed(values, inside)
        scaled = xhat * fgain_ref[...] + fbias_ref[...]
        hidden = jnp.where(inside, scaled / (1.0 + jnp.exp(-scaled)), 0.0)
        store_shifted(hp_buf, hidden)
        result = values + jnp.dot(columns_of(hp_buf), fw_ref[...], preferred_element_type=F32)
        emitted_ref[tick] = result.reshape(LINES, PAD, C)[:, 0:SIDE]
        return result

    for kr in range(3):
        for kc in range(3):
            mirrored = ((2 - kr) * 3 + 2 - kc) * C
            bwt_buf[(kr * 3 + kc) * C : (kr * 3 + kc + 1) * C] = bw_ref[mirrored : mirrored + C].T

    prepare(0)
    e_buf[:, 0:SIDE] = grad_ref[...].astype(F32)
    result = backward(0)
    pack(grad_out.at[0], result)
    pl.semaphore_wait(barrier, 2 + NY - 1 + NZ - 1)
    send_on(*grad_stream(0))
    x_buf[:, 0:SIDE] = act_ref[...].astype(F32)
    pack(act_out.at[0], forward(0))
    send_on(*act_stream(0))
    weight_terms(0)
    for tick in range(1, TICKS):
        prepare(tick)

    take(e_buf, fresh_grad_ref, grad_stream(0), 1)
    pack(grad_out.at[1], backward(1))
    send_on(*grad_stream(1))
    weight_terms(1)
    take(x_buf, fresh_act_ref, act_stream(0), 1)
    pack(act_out.at[1], forward(1))

    take(e_buf, fresh_grad_ref, grad_stream(1), 2)
    pack(grad_out.at[2], backward(2))
    send_on(*grad_stream(2))
    send_on(*act_stream(1))
    weight_terms(2)

    take(e_buf, fresh_grad_ref, grad_stream(2), 3)
    backward(3)
    weight_terms(3)

    total = total_buf.reshape(NY, NZ, BLOCK, C)

    def y_copy(part, k):
        peer = lax.rem(my_y + k, NY)
        return pltpu.make_async_remote_copy(
            src_ref=total.at[peer, :, pl.ds(part * PIECE, PIECE)],
            dst_ref=y_in.at[part, NY - 1 - k],
            send_sem=y_send.at[part, k - 1],
            recv_sem=y_recv.at[part, NY - 1 - k],
            device_id={"section": section, "dp": peer * NZ + my_z},
            device_id_type=MESH,
        )

    def z_copy(part, k):
        peer = lax.rem(my_z + k, NZ)
        return pltpu.make_async_remote_copy(
            src_ref=y_sum.at[part, peer],
            dst_ref=z_in.at[part, NZ - 1 - k],
            send_sem=z_send.at[part, k - 1],
            recv_sem=z_recv.at[part, NZ - 1 - k],
            device_id={"section": section, "dp": my_y * NZ + peer},
            device_id_type=MESH,
        )

    for part in range(PARTS):
        for k in (2, 1, 3):
            y_copy(part, k).start()

    take(x_buf, fresh_act_ref, act_stream(1), 2)
    pack(act_out.at[2], forward(2))
    send_on(*act_stream(2))

    for part in range(PARTS):
        for k in range(1, NY):
            y_copy(part, k).wait_recv()
        y_sum[part] = total[my_y, :, pl.ds(part * PIECE, PIECE)] + (
            y_in[part, 0] + y_in[part, 1] + y_in[part, 2]
        )
        for k in (4, 3, 5, 2, 6, 1, 7):
            z_copy(part, k).start()

    take(x_buf, fresh_act_ref, act_stream(2), 3)
    forward(3)

    for part in range(PARTS):
        for k in range(1, NZ):
            z_copy(part, k).wait_recv()
        block = y_sum[part, my_z]
        for k in range(NZ - 1):
            block = block + z_in[part, k]
        wgrad_ref[part * PIECE : (part + 1) * PIECE] = block * (1.0 / BATCH)

    @pl.when(section < SECTIONS - 1)
    def _():
        for tick in range(TICKS - 1):
            sender(*grad_stream(tick)).wait_send()
            sender(*act_stream(tick)).wait_send()

    for part in range(PARTS):
        for k in range(1, NY):
            y_copy(part, k).wait_send()
        for k in range(1, NZ):
            z_copy(part, k).wait_send()


def shards(
    arriving_activations,
    fresh_images,
    saved_inputs,
    arriving_gradients,
    fresh_gradients,
    feed_order,
    forward_weight,
    forward_gain,
    forward_bias,
    backward_weight,
    backward_gain,
    backward_bias,
):
    fold = (LINES, SIDE, C)
    vmem = pl.BlockSpec(memory_space=pltpu.VMEM)
    dma = pltpu.SemaphoreType.DMA
    relay = pltpu.VMEM((TICKS - 1, PACKED // 8, 8, C), F32)
    emitted, returned, block = pl.pallas_call(
        kernel,
        out_shape=(
            jax.ShapeDtypeStruct((TICKS,) + fold, F32),
            jax.ShapeDtypeStruct((TICKS,) + fold, F32),
            jax.ShapeDtypeStruct((BLOCK, C), F32),
        ),
        in_specs=[pl.BlockSpec(memory_space=pltpu.SMEM)] + [vmem] * 11,
        out_specs=(vmem, vmem, vmem),
        scratch_shapes=[
            pltpu.VMEM((LINES, PAD, C), F32),
            pltpu.VMEM((LINES, PAD, C), F32),
            pltpu.VMEM((TICKS, ROWS, C), F32),
            pltpu.VMEM((TICKS, ROWS, C), F32),
            pltpu.VMEM((TICKS, IMAGES, C), F32),
            pltpu.VMEM((TICKS, 3 * C, ROWS), BF16),
            pltpu.VMEM((TAPS * C, C), BF16),
            pltpu.VMEM((3, IMAGES, SIDE + 2, PAD, C), BF16),
            pltpu.VMEM((3, IMAGES, SIDE + 2, PAD, C), BF16),
            pltpu.VMEM((TAPS * C, C), F32),
            relay,
            relay,
            relay,
            relay,
            pltpu.VMEM((PARTS, NY - 1, NZ, PIECE, C), F32),
            pltpu.VMEM((PARTS, NZ, PIECE, C), F32),
            pltpu.VMEM((PARTS, NZ - 1, PIECE, C), F32),
            dma((TICKS - 1,)),
            dma((TICKS - 1,)),
            dma((TICKS - 1,)),
            dma((TICKS - 1,)),
            dma((PARTS, NY - 1)),
            dma((PARTS, NY - 1)),
            dma((PARTS, NZ - 1)),
            dma((PARTS, NZ - 1)),
        ],
        compiler_params=pltpu.CompilerParams(
            collective_id=0, has_side_effects=True, vmem_limit_bytes=60 * 1024 * 1024
        ),
    )(
        feed_order,
        arriving_activations.reshape(fold),
        fresh_images.reshape((TICKS - 1,) + fold),
        saved_inputs.reshape((TICKS,) + fold),
        arriving_gradients.reshape(fold),
        fresh_gradients.reshape((TICKS - 1,) + fold),
        forward_weight[0],
        forward_gain,
        forward_bias,
        backward_weight[0],
        backward_gain,
        backward_bias,
    )
    whole = (TICKS, 1, IMAGES, SIDE, SIDE, C)
    return (emitted.reshape(whole), returned.reshape(whole), block[None])


def solution(mesh):
    placed = (
        P("section", "dp", None, None, None),
        P(None, "dp", None, None, None),
        P(None, "section", "dp", None, None, None),
        P("section", "dp", None, None, None),
        P(None, "dp", None, None, None),
        P(),
        P("section", None, None),
        P("section", None),
        P("section", None),
        P("section", None, None),
        P("section", None),
        P("section", None),
    )
    return jax.shard_map(
        shards,
        mesh=mesh,
        in_specs=placed,
        out_specs=(
            P(None, "section", "dp", None, None, None),
            P(None, "section", "dp", None, None, None),
            P("section", "dp", None),
        ),
        check_vma=False,
    )
```

```python
import jax
import jax.numpy as jnp
from jax import lax
from jax.experimental import pallas as pl
from jax.experimental.pallas import tpu as pltpu
from jax.sharding import PartitionSpec as P

C = 256
HALF = 128
TAPS = 9
SIDE = 12
IMAGES = 2
PIXELS = SIDE * SIDE
NATIVE = PIXELS * 2 * IMAGES
ROWS = PIXELS * IMAGES
LINE = SIDE * 2 * IMAGES
TILES = ROWS // 8
TICKS = 4
SECTIONS = 16
GROUP = 8
NY = 4
NZ = 8
BLOCK = 72
PARTS = 3
PIECE = BLOCK // PARTS
EPS = 1e-05
COUNT = PIXELS * GROUP
BATCH = 64
MESH = pl.DeviceIdType.MESH
F32 = jnp.float32
BF16 = jnp.bfloat16


def even_pairs(shape):
    return (lax.broadcasted_iota(jnp.int32, shape, 0) & 2) == 0


def worked(native):
    upper, lower = native[:ROWS], native[ROWS:]
    even = even_pairs(upper.shape)
    first = jnp.where(even, upper, pltpu.roll(lower, 2, 0))
    second = jnp.where(even, pltpu.roll(upper, ROWS - 2, 0), lower)
    return jnp.concatenate([first, second], axis=1)


def stored(values):
    first, second = values[:, :HALF], values[:, HALF:]
    even = even_pairs(first.shape)
    upper = jnp.where(even, first, pltpu.roll(second, 2, 0))
    lower = jnp.where(even, pltpu.roll(first, ROWS - 2, 0), second)
    return jnp.concatenate([upper, lower], axis=0)


def group_mean(values):
    sums = jnp.sum(values, axis=0)
    sums = sums + pltpu.roll(sums, 4, 0)
    sums = sums + pltpu.roll(sums, 2, 0)
    lane = lax.broadcasted_iota(jnp.int32, sums.shape, 1)
    for step in (1, 2, 4):
        below = pltpu.roll(sums, step, 1)
        above = pltpu.roll(sums, C - step, 1)
        sums = sums + jnp.where((lane & step) == 0, above, below)
    return sums * (1.0 / COUNT)


def normed(values):
    centred = values - group_mean(values)
    scale = lax.rsqrt(group_mean(centred * centred) + EPS)
    return centred * scale, scale


def sideways(values):
    tiles = (SIDE // 2, SIDE // 2, 8, C)
    early = lax.broadcasted_iota(jnp.int32, (SIDE // 2, 1, 8, C), 2) < 4
    left = pltpu.roll(values, 4, 0).reshape(tiles)
    left = jnp.concatenate([jnp.where(early, 0.0, left[:, :1]), left[:, 1:]], axis=1)
    right = pltpu.roll(values, ROWS - 4, 0).reshape(tiles)
    right = jnp.concatenate([right[:, :-1], jnp.where(early, right[:, -1:], 0.0)], axis=1)
    return left.reshape(ROWS, C), values, right.reshape(ROWS, C)


def bordered(values):
    even = even_pairs((LINE, C))
    above = jnp.where(even, 0.0, pltpu.roll(values[ROWS - LINE :], 2, 0))
    below = jnp.where(even, pltpu.roll(values[:LINE], LINE - 2, 0), 0.0)
    return jnp.concatenate([above, values, below], axis=0).astype(BF16)


def columns_of(sides):
    return jnp.concatenate(
        [side[kr * LINE : kr * LINE + ROWS] for kr in range(3) for side in sides], axis=1
    )


def kernel(
    order_ref,
    act_ref,
    fresh_act_ref,
    saved_ref,
    grad_ref,
    fresh_grad_ref,
    fw_ref,
    fgain_ref,
    fbias_ref,
    bw_ref,
    bgain_ref,
    bbias_ref,
    emitted_ref,
    returned_ref,
    wgrad_ref,
    x_buf,
    e_buf,
    xhat_buf,
    slope_buf,
    scale_buf,
    hidden_buf,
    turned_buf,
    bwt_buf,
    border_buf,
    total_buf,
    act_out,
    act_in,
    grad_out,
    grad_in,
    y_in,
    y_sum,
    z_in,
    act_send,
    act_recv,
    grad_send,
    grad_recv,
    y_send,
    y_recv,
    z_send,
    z_recv,
):
    section = lax.axis_index("section")
    shard = lax.axis_index("dp")
    my_y = shard // NZ
    my_z = lax.rem(shard, NZ)

    barrier = pltpu.get_barrier_semaphore()
    for near in (lax.rem(section + 1, SECTIONS), lax.rem(section + SECTIONS - 1, SECTIONS)):
        pl.semaphore_signal(
            barrier, inc=1, device_id={"section": near, "dp": shard}, device_id_type=MESH
        )
    for k in range(1, NY):
        peer = lax.rem(my_y + k, NY) * NZ + my_z
        pl.semaphore_signal(
            barrier, inc=1, device_id={"section": section, "dp": peer}, device_id_type=MESH
        )
    for k in range(1, NZ):
        peer = my_y * NZ + lax.rem(my_z + k, NZ)
        pl.semaphore_signal(
            barrier, inc=1, device_id={"section": section, "dp": peer}, device_id_type=MESH
        )

    def sender(out, into, send, recv, tick):
        return pltpu.make_async_remote_copy(
            src_ref=out.at[tick],
            dst_ref=into.at[tick],
            send_sem=send.at[tick],
            recv_sem=recv.at[tick],
            device_id={"section": lax.rem(section + 1, SECTIONS), "dp": shard},
            device_id_type=MESH,
        )

    def send_on(*stream):
        @pl.when(section < SECTIONS - 1)
        def _():
            sender(*stream).start()

    def take(buf, fresh_ref, stream, tick):
        @pl.when(section == 0)
        def _():
            buf[...] = worked(fresh_ref[order_ref[tick - 1]].astype(F32)).reshape(TILES, 8, C)

        @pl.when(section > 0)
        def _():
            sender(*stream).wait_recv()
            buf[...] = stream[1][tick - 1]

    act_stream = lambda tick: (act_out, act_in, act_send, act_recv, tick)
    grad_stream = lambda tick: (grad_out, grad_in, grad_send, grad_recv, tick)

    def prepare(tick):
        values = worked(saved_ref[tick].astype(F32)).reshape(TILES, 8, C)
        xhat, scale = normed(values)
        gain = bgain_ref[...]
        scaled = xhat * gain + bbias_ref[...]
        gate = 1.0 / (1.0 + jnp.exp(-scaled))
        xhat_buf[tick] = xhat
        scale_buf[tick] = scale
        slope_buf[tick] = gate * (1.0 + scaled * (1.0 - gate)) * gain
        hidden_buf[tick] = scaled * gate

    def turn(tick):
        for kc, side in enumerate(sideways(hidden_buf[tick].reshape(ROWS, C))):
            turned_buf[tick, kc * C : (kc + 1) * C] = side.T.astype(BF16)

    def backward(tick):
        incoming = e_buf[...]
        sides = [bordered(side) for side in sideways(incoming.reshape(ROWS, C))]
        border_buf[...] = sides[1]
        hidden_grad = jnp.dot(columns_of(sides), bwt_buf[...], preferred_element_type=F32)
        through = hidden_grad.reshape(TILES, 8, C) * slope_buf[tick]
        xhat = xhat_buf[tick]
        level = group_mean(through)
        tilt = group_mean(through * xhat)
        return incoming + scale_buf[tick] * (through - level - xhat * tilt)

    def weight_terms(tick):
        for kr in range(3):
            shifted = border_buf[(2 - kr) * LINE : (2 - kr) * LINE + ROWS]
            term = jnp.dot(turned_buf[tick], shifted, preferred_element_type=F32)
            rows = pl.ds(kr * 3 * C, 3 * C)
            if tick == 0:
                total_buf[rows] = term
            else:
                total_buf[rows] += term

    def forward():
        values = x_buf[...]
        xhat, _ = normed(values)
        scaled = xhat * fgain_ref[...] + fbias_ref[...]
        hidden = scaled / (1.0 + jnp.exp(-scaled))
        sides = [bordered(side) for side in sideways(hidden.reshape(ROWS, C))]
        mixed = jnp.dot(columns_of(sides), fw_ref[...], preferred_element_type=F32)
        return values + mixed.reshape(TILES, 8, C)

    def store(out_ref, tick, values):
        out_ref[tick] = stored(values.reshape(ROWS, C))

    for kr in range(3):
        for kc in range(3):
            mirrored = ((2 - kr) * 3 + 2 - kc) * C
            bwt_buf[(kr * 3 + kc) * C : (kr * 3 + kc + 1) * C] = bw_ref[mirrored : mirrored + C].T

    prepare(0)
    e_buf[...] = worked(grad_ref[...].astype(F32)).reshape(TILES, 8, C)
    grad_out[0] = backward(0)
    pl.semaphore_wait(barrier, 2 + NY - 1 + NZ - 1)
    send_on(*grad_stream(0))
    x_buf[...] = worked(act_ref[...].astype(F32)).reshape(TILES, 8, C)
    act_out[0] = forward()
    send_on(*act_stream(0))
    for tick in range(1, TICKS):
        prepare(tick)
    store(returned_ref, 0, grad_out[0])
    store(emitted_ref, 0, act_out[0])
    turn(0)
    weight_terms(0)

    take(e_buf, fresh_grad_ref, grad_stream(0), 1)
    grad_out[1] = backward(1)
    send_on(*grad_stream(1))
    store(returned_ref, 1, grad_out[1])
    turn(1)
    weight_terms(1)
    take(x_buf, fresh_act_ref, act_stream(0), 1)
    act_out[1] = forward()
    store(emitted_ref, 1, act_out[1])
    turn(2)
    turn(3)

    take(e_buf, fresh_grad_ref, grad_stream(1), 2)
    grad_out[2] = backward(2)
    send_on(*grad_stream(2))
    send_on(*act_stream(1))
    store(returned_ref, 2, grad_out[2])
    weight_terms(2)

    take(e_buf, fresh_grad_ref, grad_stream(2), 3)
    store(returned_ref, 3, backward(3))
    weight_terms(3)

    total = total_buf.reshape(NY, NZ, BLOCK, C)

    def y_copy(part, k):
        peer = lax.rem(my_y + k, NY)
        return pltpu.make_async_remote_copy(
            src_ref=total.at[peer, :, pl.ds(part * PIECE, PIECE)],
            dst_ref=y_in.at[part, NY - 1 - k],
            send_sem=y_send.at[part, k - 1],
            recv_sem=y_recv.at[part, NY - 1 - k],
            device_id={"section": section, "dp": peer * NZ + my_z},
            device_id_type=MESH,
        )

    def z_copy(part, k):
        peer = lax.rem(my_z + k, NZ)
        return pltpu.make_async_remote_copy(
            src_ref=y_sum.at[part, peer],
            dst_ref=z_in.at[part, NZ - 1 - k],
            send_sem=z_send.at[part, k - 1],
            recv_sem=z_recv.at[part, NZ - 1 - k],
            device_id={"section": section, "dp": my_y * NZ + peer},
            device_id_type=MESH,
        )

    for part in range(PARTS):
        for k in (2, 1, 3):
            y_copy(part, k).start()

    take(x_buf, fresh_act_ref, act_stream(1), 2)
    act_out[2] = forward()
    send_on(*act_stream(2))
    store(emitted_ref, 2, act_out[2])

    for part in range(PARTS):
        for k in range(1, NY):
            y_copy(part, k).wait_recv()
        y_sum[part] = total[my_y, :, pl.ds(part * PIECE, PIECE)] + (
            y_in[part, 0] + y_in[part, 1] + y_in[part, 2]
        )
        for k in (4, 3, 5, 2, 6, 1, 7):
            z_copy(part, k).start()

    take(x_buf, fresh_act_ref, act_stream(2), 3)
    store(emitted_ref, 3, forward())

    for part in range(PARTS):
        for k in range(1, NZ):
            z_copy(part, k).wait_recv()
        block = y_sum[part, my_z]
        for k in range(NZ - 1):
            block = block + z_in[part, k]
        wgrad_ref[part * PIECE : (part + 1) * PIECE] = block * (1.0 / BATCH)

    @pl.when(section < SECTIONS - 1)
    def _():
        for tick in range(TICKS - 1):
            sender(*grad_stream(tick)).wait_send()
            sender(*act_stream(tick)).wait_send()

    for part in range(PARTS):
        for k in range(1, NY):
            y_copy(part, k).wait_send()
        for k in range(1, NZ):
            z_copy(part, k).wait_send()


def as_rows(images):
    lead = images.shape[:-4]
    n = len(lead)
    split = images.reshape(lead + (IMAGES, SIDE, SIDE, 2, HALF))
    turned = split.transpose(tuple(range(n)) + (n + 1, n + 2, n + 3, n, n + 4))
    return turned.reshape(lead + (NATIVE, HALF))


def as_images(rows):
    lead = rows.shape[:-2]
    n = len(lead)
    split = rows.reshape(lead + (SIDE, SIDE, 2, IMAGES, HALF))
    turned = split.transpose(tuple(range(n)) + (n + 3, n, n + 1, n + 2, n + 4))
    return turned.reshape(lead + (IMAGES, SIDE, SIDE, C))


def shards(
    arriving_activations,
    fresh_images,
    saved_inputs,
    arriving_gradients,
    fresh_gradients,
    feed_order,
    forward_weight,
    forward_gain,
    forward_bias,
    backward_weight,
    backward_gain,
    backward_bias,
):
    vmem = pl.BlockSpec(memory_space=pltpu.VMEM)
    dma = pltpu.SemaphoreType.DMA
    tile = (TILES, 8, C)
    relay = pltpu.VMEM((TICKS - 1,) + tile, F32)
    emitted, returned, block = pl.pallas_call(
        kernel,
        out_shape=(
            jax.ShapeDtypeStruct((TICKS, NATIVE, HALF), F32),
            jax.ShapeDtypeStruct((TICKS, NATIVE, HALF), F32),
            jax.ShapeDtypeStruct((BLOCK, C), F32),
        ),
        in_specs=[pl.BlockSpec(memory_space=pltpu.SMEM)] + [vmem] * 11,
        out_specs=(vmem, vmem, vmem),
        scratch_shapes=[
            pltpu.VMEM(tile, F32),
            pltpu.VMEM(tile, F32),
            pltpu.VMEM((TICKS,) + tile, F32),
            pltpu.VMEM((TICKS,) + tile, F32),
            pltpu.VMEM((TICKS, 8, C), F32),
            pltpu.VMEM((TICKS,) + tile, F32),
            pltpu.VMEM((TICKS, 3 * C, ROWS), BF16),
            pltpu.VMEM((TAPS * C, C), BF16),
            pltpu.VMEM((ROWS + 2 * LINE, C), BF16),
            pltpu.VMEM((TAPS * C, C), F32),
            relay,
            relay,
            relay,
            relay,
            pltpu.VMEM((PARTS, NY - 1, NZ, PIECE, C), F32),
            pltpu.VMEM((PARTS, NZ, PIECE, C), F32),
            pltpu.VMEM((PARTS, NZ - 1, PIECE, C), F32),
            dma((TICKS - 1,)),
            dma((TICKS - 1,)),
            dma((TICKS - 1,)),
            dma((TICKS - 1,)),
            dma((PARTS, NY - 1)),
            dma((PARTS, NY - 1)),
            dma((PARTS, NZ - 1)),
            dma((PARTS, NZ - 1)),
        ],
        compiler_params=pltpu.CompilerParams(
            collective_id=0, has_side_effects=True, vmem_limit_bytes=60 * 1024 * 1024
        ),
    )(
        feed_order,
        as_rows(arriving_activations[0]),
        as_rows(fresh_images),
        as_rows(saved_inputs[:, 0]),
        as_rows(arriving_gradients[0]),
        as_rows(fresh_gradients),
        forward_weight[0],
        forward_gain,
        forward_bias,
        backward_weight[0],
        backward_gain,
        backward_bias,
    )
    return (as_images(emitted)[:, None], as_images(returned)[:, None], block[None])


def solution(mesh):
    placed = (
        P("section", "dp", None, None, None),
        P(None, "dp", None, None, None),
        P(None, "section", "dp", None, None, None),
        P("section", "dp", None, None, None),
        P(None, "dp", None, None, None),
        P(),
        P("section", None, None),
        P("section", None),
        P("section", None),
        P("section", None, None),
        P("section", None),
        P("section", None),
    )
    return jax.shard_map(
        shards,
        mesh=mesh,
        in_specs=placed,
        out_specs=(
            P(None, "section", "dp", None, None, None),
            P(None, "section", "dp", None, None, None),
            P("section", "dp", None),
        ),
        check_vma=False,
    )
```

```python
import jax
import jax.numpy as jnp
from jax import lax
from jax.experimental import pallas as pl
from jax.experimental.pallas import tpu as pltpu
from jax.sharding import PartitionSpec as P

C = 256
HALF = 128
TAPS = 9
SIDE = 12
IMAGES = 2
PIXELS = SIDE * SIDE
NATIVE = PIXELS * 2 * IMAGES
ROWS = PIXELS * IMAGES
LINE = SIDE * 2 * IMAGES
TILES = ROWS // 8
TICKS = 4
SECTIONS = 16
GROUP = 8
NY = 4
NZ = 8
QUAD = 4
BLOCK = 72
PARTS = 3
PIECE = BLOCK // PARTS
EPS = 1e-05
COUNT = PIXELS * GROUP
BATCH = 64
MESH = pl.DeviceIdType.MESH
F32 = jnp.float32
BF16 = jnp.bfloat16


def even_pairs(shape):
    return (lax.broadcasted_iota(jnp.int32, shape, 0) & 2) == 0


def worked(native):
    upper, lower = native[:ROWS], native[ROWS:]
    even = even_pairs(upper.shape)
    first = jnp.where(even, upper, pltpu.roll(lower, 2, 0))
    second = jnp.where(even, pltpu.roll(upper, ROWS - 2, 0), lower)
    return jnp.concatenate([first, second], axis=1)


def stored(values):
    first, second = values[:, :HALF], values[:, HALF:]
    even = even_pairs(first.shape)
    upper = jnp.where(even, first, pltpu.roll(second, 2, 0))
    lower = jnp.where(even, pltpu.roll(first, ROWS - 2, 0), second)
    return jnp.concatenate([upper, lower], axis=0)


def group_mean(values):
    sums = jnp.sum(values, axis=0)
    sums = sums + pltpu.roll(sums, 4, 0)
    sums = sums + pltpu.roll(sums, 2, 0)
    lane = lax.broadcasted_iota(jnp.int32, sums.shape, 1)
    for step in (1, 2, 4):
        below = pltpu.roll(sums, step, 1)
        above = pltpu.roll(sums, C - step, 1)
        sums = sums + jnp.where((lane & step) == 0, above, below)
    return sums * (1.0 / COUNT)


def normed(values):
    centred = values - group_mean(values)
    scale = lax.rsqrt(group_mean(centred * centred) + EPS)
    return centred * scale, scale


def sideways(values):
    tiles = (SIDE // 2, SIDE // 2, 8, C)
    early = lax.broadcasted_iota(jnp.int32, (SIDE // 2, 1, 8, C), 2) < 4
    left = pltpu.roll(values, 4, 0).reshape(tiles)
    left = jnp.concatenate([jnp.where(early, 0.0, left[:, :1]), left[:, 1:]], axis=1)
    right = pltpu.roll(values, ROWS - 4, 0).reshape(tiles)
    right = jnp.concatenate([right[:, :-1], jnp.where(early, right[:, -1:], 0.0)], axis=1)
    return left.reshape(ROWS, C), values, right.reshape(ROWS, C)


def bordered(values):
    even = even_pairs((LINE, C))
    above = jnp.where(even, 0.0, pltpu.roll(values[ROWS - LINE :], 2, 0))
    below = jnp.where(even, pltpu.roll(values[:LINE], LINE - 2, 0), 0.0)
    return jnp.concatenate([above, values, below], axis=0).astype(BF16)


def columns_of(sides):
    return jnp.concatenate(
        [side[kr * LINE : kr * LINE + ROWS] for kr in range(3) for side in sides], axis=1
    )


def kernel(
    order_ref,
    act_hbm,
    fresh_act_hbm,
    saved_hbm,
    grad_hbm,
    fresh_grad_hbm,
    fw_hbm,
    fgain_ref,
    fbias_ref,
    bw_hbm,
    bgain_ref,
    bbias_ref,
    emitted_hbm,
    returned_hbm,
    wgrad_ref,
    act_ref,
    fresh_act_ref,
    saved_ref,
    grad_ref,
    fresh_grad_ref,
    fw_ref,
    bw_ref,
    emitted_ref,
    returned_ref,
    x_buf,
    e_buf,
    xhat_buf,
    slope_buf,
    scale_buf,
    hidden_buf,
    turned_buf,
    bwt_buf,
    border_buf,
    total_buf,
    act_out,
    act_in,
    grad_out,
    grad_in,
    y_in,
    y_sum,
    z_in,
    z_mid,
    far_in,
    act_send,
    act_recv,
    grad_send,
    grad_recv,
    y_send,
    y_recv,
    z_send,
    z_recv,
    far_send,
    far_recv,
    load_sem,
    emitted_sem,
    returned_sem,
):
    section = lax.axis_index("section")
    shard = lax.axis_index("dp")
    my_y = shard // NZ
    my_z = lax.rem(shard, NZ)
    my_q = my_z // QUAD
    my_w = lax.rem(my_z, QUAD)

    barrier = pltpu.get_barrier_semaphore()
    for near in (lax.rem(section + 1, SECTIONS), lax.rem(section + SECTIONS - 1, SECTIONS)):
        pl.semaphore_signal(
            barrier, inc=1, device_id={"section": near, "dp": shard}, device_id_type=MESH
        )
    for k in range(1, NY):
        peer = lax.rem(my_y + k, NY) * NZ + my_z
        pl.semaphore_signal(
            barrier, inc=1, device_id={"section": section, "dp": peer}, device_id_type=MESH
        )
    far = lax.rem(my_z + QUAD, NZ)
    for peer in [my_q * QUAD + lax.rem(my_w + k, QUAD) for k in range(1, QUAD)] + [far]:
        pl.semaphore_signal(
            barrier,
            inc=1,
            device_id={"section": section, "dp": my_y * NZ + peer},
            device_id_type=MESH,
        )

    loads = [
        pltpu.make_async_copy(source, buf, load_sem.at[i])
        for i, (source, buf) in enumerate(
            (
                (bw_hbm, bw_ref),
                (saved_hbm, saved_ref),
                (grad_hbm, grad_ref),
                (fw_hbm, fw_ref),
                (act_hbm, act_ref),
                (fresh_grad_hbm, fresh_grad_ref),
                (fresh_act_hbm, fresh_act_ref),
            )
        )
    ]
    for load in loads:
        load.start()

    def sender(out, into, send, recv, tick):
        return pltpu.make_async_remote_copy(
            src_ref=out.at[tick],
            dst_ref=into.at[tick],
            send_sem=send.at[tick],
            recv_sem=recv.at[tick],
            device_id={"section": lax.rem(section + 1, SECTIONS), "dp": shard},
            device_id_type=MESH,
        )

    def send_on(*stream):
        @pl.when(section < SECTIONS - 1)
        def _():
            sender(*stream).start()

    def sent(*stream):
        @pl.when(section < SECTIONS - 1)
        def _():
            sender(*stream).wait_send()

    def take(buf, fresh_ref, stream, tick):
        @pl.when(section == 0)
        def _():
            buf[...] = worked(fresh_ref[order_ref[tick - 1]].astype(F32)).reshape(TILES, 8, C)

        @pl.when(section > 0)
        def _():
            sender(*stream).wait_recv()
            buf[...] = stream[1][tick - 1]

    act_stream = lambda tick: (act_out, act_in, act_send, act_recv, tick)
    grad_stream = lambda tick: (grad_out, grad_in, grad_send, grad_recv, tick)

    def prepare(tick):
        values = worked(saved_ref[tick].astype(F32)).reshape(TILES, 8, C)
        xhat, scale = normed(values)
        gain = bgain_ref[...]
        scaled = xhat * gain + bbias_ref[...]
        gate = 1.0 / (1.0 + jnp.exp(-scaled))
        xhat_buf[tick] = xhat
        scale_buf[tick] = scale
        slope_buf[tick] = gate * (1.0 + scaled * (1.0 - gate)) * gain
        hidden_buf[tick] = scaled * gate

    def turn(tick):
        for kc, side in enumerate(sideways(hidden_buf[tick].reshape(ROWS, C))):
            turned_buf[tick, kc * C : (kc + 1) * C] = side.T.astype(BF16)

    def backward(tick):
        incoming = e_buf[...]
        sides = [bordered(side) for side in sideways(incoming.reshape(ROWS, C))]
        border_buf[...] = sides[1]
        hidden_grad = jnp.dot(columns_of(sides), bwt_buf[...], preferred_element_type=F32)
        through = hidden_grad.reshape(TILES, 8, C) * slope_buf[tick]
        xhat = xhat_buf[tick]
        level = group_mean(through)
        tilt = group_mean(through * xhat)
        return incoming + scale_buf[tick] * (through - level - xhat * tilt)

    def weight_terms(tick):
        for kr in range(3):
            shifted = border_buf[(2 - kr) * LINE : (2 - kr) * LINE + ROWS]
            term = jnp.dot(turned_buf[tick], shifted, preferred_element_type=F32)
            rows = pl.ds(kr * 3 * C, 3 * C)
            if tick == 0:
                total_buf[rows] = term
            else:
                total_buf[rows] += term

    def forward():
        values = x_buf[...]
        xhat, _ = normed(values)
        scaled = xhat * fgain_ref[...] + fbias_ref[...]
        hidden = scaled / (1.0 + jnp.exp(-scaled))
        sides = [bordered(side) for side in sideways(hidden.reshape(ROWS, C))]
        mixed = jnp.dot(columns_of(sides), fw_ref[...], preferred_element_type=F32)
        return values + mixed.reshape(TILES, 8, C)

    def written(side, tick):
        buf, out, sem = side
        return pltpu.make_async_copy(buf.at[tick], out.at[tick], sem.at[tick])

    def store(side, tick, values):
        side[0][tick] = stored(values.reshape(ROWS, C))
        written(side, tick).start()

    emitted_side = (emitted_ref, emitted_hbm, emitted_sem)
    returned_side = (returned_ref, returned_hbm, returned_sem)

    loads[0].wait()
    for kr in range(3):
        for kc in range(3):
            mirrored = ((2 - kr) * 3 + 2 - kc) * C
            bwt_buf[(kr * 3 + kc) * C : (kr * 3 + kc + 1) * C] = bw_ref[mirrored : mirrored + C].T

    loads[1].wait()
    prepare(0)
    loads[2].wait()
    e_buf[...] = worked(grad_ref[...].astype(F32)).reshape(TILES, 8, C)
    grad_out[0] = backward(0)
    loads[3].wait()
    loads[4].wait()
    x_buf[...] = worked(act_ref[...].astype(F32)).reshape(TILES, 8, C)
    act_out[0] = forward()
    pl.semaphore_wait(barrier, 2 + NY - 1 + QUAD)
    send_on(*grad_stream(0))
    store(returned_side, 0, grad_out[0])
    turn(0)
    weight_terms(0)
    for tick in range(1, TICKS):
        prepare(tick)
    turn(1)
    turn(2)
    turn(3)
    sent(*grad_stream(0))
    send_on(*act_stream(0))
    store(emitted_side, 0, act_out[0])
    loads[5].wait()
    loads[6].wait()

    take(e_buf, fresh_grad_ref, grad_stream(0), 1)
    grad_out[1] = backward(1)
    sent(*act_stream(0))
    send_on(*grad_stream(1))
    store(returned_side, 1, grad_out[1])
    weight_terms(1)
    take(x_buf, fresh_act_ref, act_stream(0), 1)
    act_out[1] = forward()
    store(emitted_side, 1, act_out[1])

    take(e_buf, fresh_grad_ref, grad_stream(1), 2)
    grad_out[2] = backward(2)
    send_on(*grad_stream(2))
    store(returned_side, 2, grad_out[2])
    weight_terms(2)
    sent(*grad_stream(2))
    send_on(*act_stream(1))

    take(e_buf, fresh_grad_ref, grad_stream(2), 3)
    store(returned_side, 3, backward(3))
    weight_terms(3)

    total = total_buf.reshape(NY, NZ, BLOCK, C)

    def y_copy(part, k):
        peer = lax.rem(my_y + k, NY)
        return pltpu.make_async_remote_copy(
            src_ref=total.at[peer, :, pl.ds(part * PIECE, PIECE)],
            dst_ref=y_in.at[part, NY - 1 - k],
            send_sem=y_send.at[part, k - 1],
            recv_sem=y_recv.at[part, NY - 1 - k],
            device_id={"section": section, "dp": peer * NZ + my_z},
            device_id_type=MESH,
        )

    def z_copy(part, k):
        peer = lax.rem(my_w + k, QUAD)
        return pltpu.make_async_remote_copy(
            src_ref=y_sum.at[part, :, peer],
            dst_ref=z_in.at[part, QUAD - 1 - k],
            send_sem=z_send.at[part, k - 1],
            recv_sem=z_recv.at[part, QUAD - 1 - k],
            device_id={"section": section, "dp": my_y * NZ + my_q * QUAD + peer},
            device_id_type=MESH,
        )

    def far_copy(part):
        return pltpu.make_async_remote_copy(
            src_ref=z_mid.at[part, 1 - my_q],
            dst_ref=far_in.at[part],
            send_sem=far_send.at[part],
            recv_sem=far_recv.at[part],
            device_id={"section": section, "dp": my_y * NZ + far},
            device_id_type=MESH,
        )

    def y_done(part):
        for k in range(1, NY):
            y_copy(part, k).wait_recv()
        piece = total[my_y, :, pl.ds(part * PIECE, PIECE)] + (
            y_in[part, 0] + y_in[part, 1] + y_in[part, 2]
        )
        y_sum[part] = piece.reshape(NZ // QUAD, QUAD, PIECE, C)
        for k in (2, 1, 3):
            z_copy(part, k).start()

    def y_start(part):
        if part > 0:
            for k in range(1, NY):
                y_copy(part - 1, k).wait_send()
        for k in (2, 1, 3):
            y_copy(part, k).start()

    y_start(0)
    take(x_buf, fresh_act_ref, act_stream(1), 2)
    act_out[2] = forward()
    sent(*act_stream(1))
    send_on(*act_stream(2))
    store(emitted_side, 2, act_out[2])
    for part in range(1, PARTS):
        y_start(part)
        y_done(part - 1)

    take(x_buf, fresh_act_ref, act_stream(2), 3)
    store(emitted_side, 3, forward())

    y_done(PARTS - 1)

    for part in range(PARTS):
        for k in range(1, QUAD):
            z_copy(part, k).wait_recv()
        z_mid[part] = y_sum[part, :, my_w] + (z_in[part, 0] + z_in[part, 1] + z_in[part, 2])
        far_copy(part).start()

    for part in range(PARTS):
        far_copy(part).wait_recv()
        block = z_mid[part, my_q] + far_in[part]
        wgrad_ref[part * PIECE : (part + 1) * PIECE] = block * (1.0 / BATCH)

    for stream in (grad_stream(1), act_stream(2)):
        sent(*stream)

    for k in range(1, NY):
        y_copy(PARTS - 1, k).wait_send()
    for part in range(PARTS):
        for k in range(1, QUAD):
            z_copy(part, k).wait_send()
        far_copy(part).wait_send()

    for tick in range(TICKS):
        written(emitted_side, tick).wait()
        written(returned_side, tick).wait()


def as_rows(images):
    lead = images.shape[:-4]
    n = len(lead)
    split = images.reshape(lead + (IMAGES, SIDE, SIDE, 2, HALF))
    turned = split.transpose(tuple(range(n)) + (n + 1, n + 2, n + 3, n, n + 4))
    return turned.reshape(lead + (NATIVE, HALF))


def as_images(rows):
    lead = rows.shape[:-2]
    n = len(lead)
    split = rows.reshape(lead + (SIDE, SIDE, 2, IMAGES, HALF))
    turned = split.transpose(tuple(range(n)) + (n + 3, n, n + 1, n + 2, n + 4))
    return turned.reshape(lead + (IMAGES, SIDE, SIDE, C))


def shards(
    arriving_activations,
    fresh_images,
    saved_inputs,
    arriving_gradients,
    fresh_gradients,
    feed_order,
    forward_weight,
    forward_gain,
    forward_bias,
    backward_weight,
    backward_gain,
    backward_bias,
):
    vmem = pl.BlockSpec(memory_space=pltpu.VMEM)
    whole = pl.BlockSpec(memory_space=pl.ANY)
    dma = pltpu.SemaphoreType.DMA
    tile = (TILES, 8, C)
    relay = pltpu.VMEM((TICKS - 1,) + tile, F32)
    emitted, returned, block = pl.pallas_call(
        kernel,
        out_shape=(
            jax.ShapeDtypeStruct((TICKS, NATIVE, HALF), F32),
            jax.ShapeDtypeStruct((TICKS, NATIVE, HALF), F32),
            jax.ShapeDtypeStruct((BLOCK, C), F32),
        ),
        in_specs=[pl.BlockSpec(memory_space=pltpu.SMEM)]
        + [whole] * 6
        + [vmem] * 2
        + [whole]
        + [vmem] * 2,
        out_specs=(whole, whole, vmem),
        scratch_shapes=[
            pltpu.VMEM((NATIVE, HALF), BF16),
            pltpu.VMEM((TICKS - 1, NATIVE, HALF), BF16),
            pltpu.VMEM((TICKS, NATIVE, HALF), BF16),
            pltpu.VMEM((NATIVE, HALF), BF16),
            pltpu.VMEM((TICKS - 1, NATIVE, HALF), BF16),
            pltpu.VMEM((TAPS * C, C), BF16),
            pltpu.VMEM((TAPS * C, C), BF16),
            pltpu.VMEM((TICKS, NATIVE, HALF), F32),
            pltpu.VMEM((TICKS, NATIVE, HALF), F32),
            pltpu.VMEM(tile, F32),
            pltpu.VMEM(tile, F32),
            pltpu.VMEM((TICKS,) + tile, F32),
            pltpu.VMEM((TICKS,) + tile, F32),
            pltpu.VMEM((TICKS, 8, C), F32),
            pltpu.VMEM((TICKS,) + tile, F32),
            pltpu.VMEM((TICKS, 3 * C, ROWS), BF16),
            pltpu.VMEM((TAPS * C, C), BF16),
            pltpu.VMEM((ROWS + 2 * LINE, C), BF16),
            pltpu.VMEM((TAPS * C, C), F32),
            relay,
            relay,
            relay,
            relay,
            pltpu.VMEM((PARTS, NY - 1, NZ, PIECE, C), F32),
            pltpu.VMEM((PARTS, NZ // QUAD, QUAD, PIECE, C), F32),
            pltpu.VMEM((PARTS, QUAD - 1, NZ // QUAD, PIECE, C), F32),
            pltpu.VMEM((PARTS, NZ // QUAD, PIECE, C), F32),
            pltpu.VMEM((PARTS, PIECE, C), F32),
            dma((TICKS - 1,)),
            dma((TICKS - 1,)),
            dma((TICKS - 1,)),
            dma((TICKS - 1,)),
            dma((PARTS, NY - 1)),
            dma((PARTS, NY - 1)),
            dma((PARTS, QUAD - 1)),
            dma((PARTS, QUAD - 1)),
            dma((PARTS,)),
            dma((PARTS,)),
            dma((7,)),
            dma((TICKS,)),
            dma((TICKS,)),
        ],
        compiler_params=pltpu.CompilerParams(
            collective_id=0, has_side_effects=True, vmem_limit_bytes=60 * 1024 * 1024
        ),
    )(
        feed_order,
        as_rows(arriving_activations[0]),
        as_rows(fresh_images),
        as_rows(saved_inputs[:, 0]),
        as_rows(arriving_gradients[0]),
        as_rows(fresh_gradients),
        forward_weight[0],
        forward_gain,
        forward_bias,
        backward_weight[0],
        backward_gain,
        backward_bias,
    )
    return (as_images(emitted)[:, None], as_images(returned)[:, None], block[None])


def solution(mesh):
    placed = (
        P("section", "dp", None, None, None),
        P(None, "dp", None, None, None),
        P(None, "section", "dp", None, None, None),
        P("section", "dp", None, None, None),
        P(None, "dp", None, None, None),
        P(),
        P("section", None, None),
        P("section", None),
        P("section", None),
        P("section", None, None),
        P("section", None),
        P("section", None),
    )
    return jax.shard_map(
        shards,
        mesh=mesh,
        in_specs=placed,
        out_specs=(
            P(None, "section", "dp", None, None, None),
            P(None, "section", "dp", None, None, None),
            P("section", "dp", None),
        ),
        check_vma=False,
    )
```

```python
import jax
import jax.numpy as jnp
from jax import lax
from jax.experimental import pallas as pl
from jax.experimental.pallas import tpu as pltpu
from jax.sharding import PartitionSpec as P

C = 256
HALF = 128
TAPS = 9
SIDE = 12
IMAGES = 2
PIXELS = SIDE * SIDE
NATIVE = PIXELS * 2 * IMAGES
ROWS = PIXELS * IMAGES
LINE = SIDE * 2 * IMAGES
TILES = ROWS // 8
TICKS = 4
SECTIONS = 16
GROUP = 8
NY = 4
NZ = 8
QUAD = 4
BLOCK = 72
PARTS = 3
PIECE = BLOCK // PARTS
EPS = 1e-05
COUNT = PIXELS * GROUP
BATCH = 64
MESH = pl.DeviceIdType.MESH
F32 = jnp.float32
BF16 = jnp.bfloat16


def even_pairs(shape):
    return (lax.broadcasted_iota(jnp.int32, shape, 0) & 2) == 0


def worked(native):
    upper, lower = native[:ROWS], native[ROWS:]
    even = even_pairs(upper.shape)
    first = jnp.where(even, upper, pltpu.roll(lower, 2, 0))
    second = jnp.where(even, pltpu.roll(upper, ROWS - 2, 0), lower)
    return jnp.concatenate([first, second], axis=1)


def stored(values):
    first, second = values[:, :HALF], values[:, HALF:]
    even = even_pairs(first.shape)
    upper = jnp.where(even, first, pltpu.roll(second, 2, 0))
    lower = jnp.where(even, pltpu.roll(first, ROWS - 2, 0), second)
    return jnp.concatenate([upper, lower], axis=0)


def group_mean(values):
    sums = jnp.sum(values, axis=0)
    sums = sums + pltpu.roll(sums, 4, 0)
    sums = sums + pltpu.roll(sums, 2, 0)
    lane = lax.broadcasted_iota(jnp.int32, sums.shape, 1)
    for step in (1, 2, 4):
        below = pltpu.roll(sums, step, 1)
        above = pltpu.roll(sums, C - step, 1)
        sums = sums + jnp.where((lane & step) == 0, above, below)
    return sums * (1.0 / COUNT)


def normed(values):
    centred = values - group_mean(values)
    scale = lax.rsqrt(group_mean(centred * centred) + EPS)
    return centred * scale, scale


def sideways(values):
    tiles = (SIDE // 2, SIDE // 2, 8, C)
    early = lax.broadcasted_iota(jnp.int32, (SIDE // 2, 1, 8, C), 2) < 4
    left = pltpu.roll(values, 4, 0).reshape(tiles)
    left = jnp.concatenate([jnp.where(early, 0.0, left[:, :1]), left[:, 1:]], axis=1)
    right = pltpu.roll(values, ROWS - 4, 0).reshape(tiles)
    right = jnp.concatenate([right[:, :-1], jnp.where(early, right[:, -1:], 0.0)], axis=1)
    return left.reshape(ROWS, C), values, right.reshape(ROWS, C)


def bordered(values):
    even = even_pairs((LINE, C))
    above = jnp.where(even, 0.0, pltpu.roll(values[ROWS - LINE :], 2, 0))
    below = jnp.where(even, pltpu.roll(values[:LINE], LINE - 2, 0), 0.0)
    return jnp.concatenate([above, values, below], axis=0).astype(BF16)


def columns_of(sides):
    return jnp.concatenate(
        [side[kr * LINE : kr * LINE + ROWS] for kr in range(3) for side in sides], axis=1
    )


def kernel(
    order_ref,
    act_hbm,
    fresh_act_hbm,
    saved_hbm,
    grad_hbm,
    fresh_grad_hbm,
    fw_hbm,
    fgain_ref,
    fbias_ref,
    bw_hbm,
    bgain_ref,
    bbias_ref,
    emitted_hbm,
    returned_hbm,
    wgrad_ref,
    act_ref,
    fresh_act_ref,
    saved_ref,
    grad_ref,
    fresh_grad_ref,
    fw_ref,
    bw_ref,
    emitted_ref,
    returned_ref,
    x_buf,
    e_buf,
    xhat_buf,
    slope_buf,
    scale_buf,
    hidden_buf,
    turned_buf,
    bwt_buf,
    border_buf,
    total_buf,
    act_out,
    act_in,
    grad_out,
    grad_in,
    y_in,
    y_sum,
    z_in,
    z_mid,
    far_in,
    act_send,
    act_recv,
    grad_send,
    grad_recv,
    y_send,
    y_recv,
    z_send,
    z_recv,
    far_send,
    far_recv,
    load_sem,
    emitted_sem,
    returned_sem,
):
    section = lax.axis_index("section")
    shard = lax.axis_index("dp")
    my_y = shard // NZ
    my_z = lax.rem(shard, NZ)
    my_q = my_z // QUAD
    my_w = lax.rem(my_z, QUAD)

    barrier = pltpu.get_barrier_semaphore()
    for near in (lax.rem(section + 1, SECTIONS), lax.rem(section + SECTIONS - 1, SECTIONS)):
        pl.semaphore_signal(
            barrier, inc=1, device_id={"section": near, "dp": shard}, device_id_type=MESH
        )
    for k in range(1, NY):
        peer = lax.rem(my_y + k, NY) * NZ + my_z
        pl.semaphore_signal(
            barrier, inc=1, device_id={"section": section, "dp": peer}, device_id_type=MESH
        )
    far = lax.rem(my_z + QUAD, NZ)
    for peer in [my_q * QUAD + lax.rem(my_w + k, QUAD) for k in range(1, QUAD)] + [far]:
        pl.semaphore_signal(
            barrier,
            inc=1,
            device_id={"section": section, "dp": my_y * NZ + peer},
            device_id_type=MESH,
        )

    loads = [
        pltpu.make_async_copy(source, buf, load_sem.at[i])
        for i, (source, buf) in enumerate(
            (
                (bw_hbm, bw_ref),
                (saved_hbm, saved_ref),
                (grad_hbm, grad_ref),
                (fw_hbm, fw_ref),
                (act_hbm, act_ref),
                (fresh_grad_hbm, fresh_grad_ref),
                (fresh_act_hbm, fresh_act_ref),
            )
        )
    ]
    for load in loads:
        load.start()

    def sender(out, into, send, recv, tick):
        return pltpu.make_async_remote_copy(
            src_ref=out.at[tick],
            dst_ref=into.at[tick],
            send_sem=send.at[tick],
            recv_sem=recv.at[tick],
            device_id={"section": lax.rem(section + 1, SECTIONS), "dp": shard},
            device_id_type=MESH,
        )

    def send_on(*stream):
        @pl.when(section < SECTIONS - 1)
        def _():
            sender(*stream).start()

    def send_from(core, *stream):
        @pl.when(jnp.logical_and(section < SECTIONS - 1, lax.rem(section, 2) == core))
        def _():
            sender(*stream).start()

    def sent(*stream):
        @pl.when(section < SECTIONS - 1)
        def _():
            sender(*stream).wait_send()

    def take(buf, fresh_ref, stream, tick):
        @pl.when(section == 0)
        def _():
            buf[...] = worked(fresh_ref[order_ref[tick - 1]].astype(F32)).reshape(TILES, 8, C)

        @pl.when(section > 0)
        def _():
            sender(*stream).wait_recv()
            buf[...] = stream[1][tick - 1]

    act_stream = lambda tick: (act_out, act_in, act_send, act_recv, tick)
    grad_stream = lambda tick: (grad_out, grad_in, grad_send, grad_recv, tick)

    def prepare(tick):
        values = worked(saved_ref[tick].astype(F32)).reshape(TILES, 8, C)
        xhat, scale = normed(values)
        gain = bgain_ref[...]
        scaled = xhat * gain + bbias_ref[...]
        gate = 1.0 / (1.0 + jnp.exp(-scaled))
        xhat_buf[tick] = xhat
        scale_buf[tick] = scale
        slope_buf[tick] = gate * (1.0 + scaled * (1.0 - gate)) * gain
        hidden_buf[tick] = scaled * gate

    def turn(tick):
        for kc, side in enumerate(sideways(hidden_buf[tick].reshape(ROWS, C))):
            turned_buf[tick, kc * C : (kc + 1) * C] = side.T.astype(BF16)

    def backward(tick):
        incoming = e_buf[...]
        sides = [bordered(side) for side in sideways(incoming.reshape(ROWS, C))]
        border_buf[...] = sides[1]
        hidden_grad = jnp.dot(columns_of(sides), bwt_buf[...], preferred_element_type=F32)
        through = hidden_grad.reshape(TILES, 8, C) * slope_buf[tick]
        xhat = xhat_buf[tick]
        level = group_mean(through)
        tilt = group_mean(through * xhat)
        return incoming + scale_buf[tick] * (through - level - xhat * tilt)

    def weight_terms(tick):
        for kr in range(3):
            shifted = border_buf[(2 - kr) * LINE : (2 - kr) * LINE + ROWS]
            term = jnp.dot(turned_buf[tick], shifted, preferred_element_type=F32)
            rows = pl.ds(kr * 3 * C, 3 * C)
            if tick == 0:
                total_buf[rows] = term
            else:
                total_buf[rows] += term

    def forward():
        values = x_buf[...]
        xhat, _ = normed(values)
        scaled = xhat * fgain_ref[...] + fbias_ref[...]
        hidden = scaled / (1.0 + jnp.exp(-scaled))
        sides = [bordered(side) for side in sideways(hidden.reshape(ROWS, C))]
        mixed = jnp.dot(columns_of(sides), fw_ref[...], preferred_element_type=F32)
        return values + mixed.reshape(TILES, 8, C)

    def written(side, tick):
        buf, out, sem = side
        return pltpu.make_async_copy(buf.at[tick], out.at[tick], sem.at[tick])

    def store(side, tick, values):
        side[0][tick] = stored(values.reshape(ROWS, C))
        written(side, tick).start()

    emitted_side = (emitted_ref, emitted_hbm, emitted_sem)
    returned_side = (returned_ref, returned_hbm, returned_sem)

    loads[0].wait()
    for kr in range(3):
        for kc in range(3):
            mirrored = ((2 - kr) * 3 + 2 - kc) * C
            bwt_buf[(kr * 3 + kc) * C : (kr * 3 + kc + 1) * C] = bw_ref[mirrored : mirrored + C].T

    loads[1].wait()
    prepare(0)
    loads[2].wait()
    e_buf[...] = worked(grad_ref[...].astype(F32)).reshape(TILES, 8, C)
    grad_out[0] = backward(0)
    loads[3].wait()
    loads[4].wait()
    x_buf[...] = worked(act_ref[...].astype(F32)).reshape(TILES, 8, C)
    act_out[0] = forward()
    pl.semaphore_wait(barrier, 2 + NY - 1 + QUAD)
    send_on(*grad_stream(0))
    send_from(0, *act_stream(0))
    store(returned_side, 0, grad_out[0])
    store(emitted_side, 0, act_out[0])
    prepare(1)
    loads[5].wait()
    loads[6].wait()
    turn(0)
    weight_terms(0)

    take(e_buf, fresh_grad_ref, grad_stream(0), 1)
    grad_out[1] = backward(1)
    sent(*grad_stream(0))
    send_on(*grad_stream(1))
    store(returned_side, 1, grad_out[1])
    turn(1)
    weight_terms(1)
    for tick in (2, 3):
        prepare(tick)
        turn(tick)
    take(e_buf, fresh_grad_ref, grad_stream(1), 2)
    grad_out[2] = backward(2)
    sent(*grad_stream(1))
    send_on(*grad_stream(2))
    store(returned_side, 2, grad_out[2])
    weight_terms(2)

    take(e_buf, fresh_grad_ref, grad_stream(2), 3)
    store(returned_side, 3, backward(3))
    weight_terms(3)

    total = total_buf.reshape(NY, NZ, BLOCK, C)

    def y_copy(part, k):
        peer = lax.rem(my_y + k, NY)
        return pltpu.make_async_remote_copy(
            src_ref=total.at[peer, :, pl.ds(part * PIECE, PIECE)],
            dst_ref=y_in.at[part, NY - 1 - k],
            send_sem=y_send.at[part, k - 1],
            recv_sem=y_recv.at[part, NY - 1 - k],
            device_id={"section": section, "dp": peer * NZ + my_z},
            device_id_type=MESH,
        )

    def z_copy(part, k):
        peer = lax.rem(my_w + k, QUAD)
        return pltpu.make_async_remote_copy(
            src_ref=y_sum.at[part, :, peer],
            dst_ref=z_in.at[part, QUAD - 1 - k],
            send_sem=z_send.at[part, k - 1],
            recv_sem=z_recv.at[part, QUAD - 1 - k],
            device_id={"section": section, "dp": my_y * NZ + my_q * QUAD + peer},
            device_id_type=MESH,
        )

    def far_copy(part):
        return pltpu.make_async_remote_copy(
            src_ref=z_mid.at[part, 1 - my_q],
            dst_ref=far_in.at[part],
            send_sem=far_send.at[part],
            recv_sem=far_recv.at[part],
            device_id={"section": section, "dp": my_y * NZ + far},
            device_id_type=MESH,
        )

    def y_done(part):
        for k in range(1, NY):
            y_copy(part, k).wait_recv()
        piece = total[my_y, :, pl.ds(part * PIECE, PIECE)] + (
            y_in[part, 0] + y_in[part, 1] + y_in[part, 2]
        )
        y_sum[part] = piece.reshape(NZ // QUAD, QUAD, PIECE, C)
        for k in (2, 1, 3):
            z_copy(part, k).start()

    def y_start(part):
        if part > 0:
            for k in range(1, NY):
                y_copy(part - 1, k).wait_send()
        for k in (2, 1, 3):
            y_copy(part, k).start()

    y_start(0)
    sent(*grad_stream(2))
    send_from(1, *act_stream(0))
    take(x_buf, fresh_act_ref, act_stream(0), 1)
    act_out[1] = forward()
    send_from(0, *act_stream(1))
    store(emitted_side, 1, act_out[1])
    y_start(1)
    y_done(0)
    sent(*act_stream(0))
    send_from(1, *act_stream(1))
    y_start(2)
    y_done(1)
    take(x_buf, fresh_act_ref, act_stream(1), 2)
    act_out[2] = forward()
    sent(*act_stream(1))
    send_on(*act_stream(2))
    store(emitted_side, 2, act_out[2])
    y_done(2)
    for part in range(PARTS):
        for k in range(1, QUAD):
            z_copy(part, k).wait_recv()
        z_mid[part] = y_sum[part, :, my_w] + (z_in[part, 0] + z_in[part, 1] + z_in[part, 2])
        far_copy(part).start()

    take(x_buf, fresh_act_ref, act_stream(2), 3)
    store(emitted_side, 3, forward())

    for part in range(PARTS):
        far_copy(part).wait_recv()
        block = z_mid[part, my_q] + far_in[part]
        wgrad_ref[part * PIECE : (part + 1) * PIECE] = block * (1.0 / BATCH)

    sent(*act_stream(2))

    for k in range(1, NY):
        y_copy(PARTS - 1, k).wait_send()
    for part in range(PARTS):
        for k in range(1, QUAD):
            z_copy(part, k).wait_send()
        far_copy(part).wait_send()

    for tick in range(TICKS):
        written(emitted_side, tick).wait()
        written(returned_side, tick).wait()


def as_rows(images):
    lead = images.shape[:-4]
    n = len(lead)
    split = images.reshape(lead + (IMAGES, SIDE, SIDE, 2, HALF))
    turned = split.transpose(tuple(range(n)) + (n + 1, n + 2, n + 3, n, n + 4))
    return turned.reshape(lead + (NATIVE, HALF))


def as_images(rows):
    lead = rows.shape[:-2]
    n = len(lead)
    split = rows.reshape(lead + (SIDE, SIDE, 2, IMAGES, HALF))
    turned = split.transpose(tuple(range(n)) + (n + 3, n, n + 1, n + 2, n + 4))
    return turned.reshape(lead + (IMAGES, SIDE, SIDE, C))


def shards(
    arriving_activations,
    fresh_images,
    saved_inputs,
    arriving_gradients,
    fresh_gradients,
    feed_order,
    forward_weight,
    forward_gain,
    forward_bias,
    backward_weight,
    backward_gain,
    backward_bias,
):
    vmem = pl.BlockSpec(memory_space=pltpu.VMEM)
    whole = pl.BlockSpec(memory_space=pl.ANY)
    dma = pltpu.SemaphoreType.DMA
    tile = (TILES, 8, C)
    relay = pltpu.VMEM((TICKS - 1,) + tile, F32)
    emitted, returned, block = pl.pallas_call(
        kernel,
        out_shape=(
            jax.ShapeDtypeStruct((TICKS, NATIVE, HALF), F32),
            jax.ShapeDtypeStruct((TICKS, NATIVE, HALF), F32),
            jax.ShapeDtypeStruct((BLOCK, C), F32),
        ),
        in_specs=[pl.BlockSpec(memory_space=pltpu.SMEM)]
        + [whole] * 6
        + [vmem] * 2
        + [whole]
        + [vmem] * 2,
        out_specs=(whole, whole, vmem),
        scratch_shapes=[
            pltpu.VMEM((NATIVE, HALF), BF16),
            pltpu.VMEM((TICKS - 1, NATIVE, HALF), BF16),
            pltpu.VMEM((TICKS, NATIVE, HALF), BF16),
            pltpu.VMEM((NATIVE, HALF), BF16),
            pltpu.VMEM((TICKS - 1, NATIVE, HALF), BF16),
            pltpu.VMEM((TAPS * C, C), BF16),
            pltpu.VMEM((TAPS * C, C), BF16),
            pltpu.VMEM((TICKS, NATIVE, HALF), F32),
            pltpu.VMEM((TICKS, NATIVE, HALF), F32),
            pltpu.VMEM(tile, F32),
            pltpu.VMEM(tile, F32),
            pltpu.VMEM((TICKS,) + tile, F32),
            pltpu.VMEM((TICKS,) + tile, F32),
            pltpu.VMEM((TICKS, 8, C), F32),
            pltpu.VMEM((TICKS,) + tile, F32),
            pltpu.VMEM((TICKS, 3 * C, ROWS), BF16),
            pltpu.VMEM((TAPS * C, C), BF16),
            pltpu.VMEM((ROWS + 2 * LINE, C), BF16),
            pltpu.VMEM((TAPS * C, C), F32),
            relay,
            relay,
            relay,
            relay,
            pltpu.VMEM((PARTS, NY - 1, NZ, PIECE, C), F32),
            pltpu.VMEM((PARTS, NZ // QUAD, QUAD, PIECE, C), F32),
            pltpu.VMEM((PARTS, QUAD - 1, NZ // QUAD, PIECE, C), F32),
            pltpu.VMEM((PARTS, NZ // QUAD, PIECE, C), F32),
            pltpu.VMEM((PARTS, PIECE, C), F32),
            dma((TICKS - 1,)),
            dma((TICKS - 1,)),
            dma((TICKS - 1,)),
            dma((TICKS - 1,)),
            dma((PARTS, NY - 1)),
            dma((PARTS, NY - 1)),
            dma((PARTS, QUAD - 1)),
            dma((PARTS, QUAD - 1)),
            dma((PARTS,)),
            dma((PARTS,)),
            dma((7,)),
            dma((TICKS,)),
            dma((TICKS,)),
        ],
        compiler_params=pltpu.CompilerParams(
            collective_id=0, has_side_effects=True, vmem_limit_bytes=60 * 1024 * 1024
        ),
    )(
        feed_order,
        as_rows(arriving_activations[0]),
        as_rows(fresh_images),
        as_rows(saved_inputs[:, 0]),
        as_rows(arriving_gradients[0]),
        as_rows(fresh_gradients),
        forward_weight[0],
        forward_gain,
        forward_bias,
        backward_weight[0],
        backward_gain,
        backward_bias,
    )
    return (as_images(emitted)[:, None], as_images(returned)[:, None], block[None])


def solution(mesh):
    placed = (
        P("section", "dp", None, None, None),
        P(None, "dp", None, None, None),
        P(None, "section", "dp", None, None, None),
        P("section", "dp", None, None, None),
        P(None, "dp", None, None, None),
        P(),
        P("section", None, None),
        P("section", None),
        P("section", None),
        P("section", None, None),
        P("section", None),
        P("section", None),
    )
    return jax.shard_map(
        shards,
        mesh=mesh,
        in_specs=placed,
        out_specs=(
            P(None, "section", "dp", None, None, None),
            P(None, "section", "dp", None, None, None),
            P("section", "dp", None),
        ),
        check_vma=False,
    )
```

```python
import jax
import jax.numpy as jnp
from jax import lax
from jax.experimental import pallas as pl
from jax.experimental.pallas import tpu as pltpu
from jax.sharding import PartitionSpec as P

C = 256
HALF = 128
TAPS = 9
SIDE = 12
IMAGES = 2
PIXELS = SIDE * SIDE
NATIVE = PIXELS * 2 * IMAGES
ROWS = PIXELS * IMAGES
LINE = SIDE * 2 * IMAGES
TILES = ROWS // 8
TICKS = 4
SECTIONS = 16
GROUP = 8
NY = 4
NZ = 8
QUAD = 4
BLOCK = 72
PARTS = 3
PIECE = BLOCK // PARTS
EPS = 1e-05
COUNT = PIXELS * GROUP
BATCH = 64
MESH = pl.DeviceIdType.MESH
F32 = jnp.float32
BF16 = jnp.bfloat16


def even_pairs(shape):
    return (lax.broadcasted_iota(jnp.int32, shape, 0) & 2) == 0


def worked(native):
    upper, lower = native[:ROWS], native[ROWS:]
    even = even_pairs(upper.shape)
    first = jnp.where(even, upper, pltpu.roll(lower, 2, 0))
    second = jnp.where(even, pltpu.roll(upper, ROWS - 2, 0), lower)
    return jnp.concatenate([first, second], axis=1)


def stored(values):
    first, second = values[:, :HALF], values[:, HALF:]
    even = even_pairs(first.shape)
    upper = jnp.where(even, first, pltpu.roll(second, 2, 0))
    lower = jnp.where(even, pltpu.roll(first, ROWS - 2, 0), second)
    return jnp.concatenate([upper, lower], axis=0)


def group_mean(values):
    sums = jnp.sum(values, axis=0)
    sums = sums + pltpu.roll(sums, 4, 0)
    sums = sums + pltpu.roll(sums, 2, 0)
    lane = lax.broadcasted_iota(jnp.int32, sums.shape, 1)
    for step in (1, 2, 4):
        below = pltpu.roll(sums, step, 1)
        above = pltpu.roll(sums, C - step, 1)
        sums = sums + jnp.where((lane & step) == 0, above, below)
    return sums * (1.0 / COUNT)


def normed(values):
    centred = values - group_mean(values)
    scale = lax.rsqrt(group_mean(centred * centred) + EPS)
    return centred * scale, scale


def sideways(values):
    tiles = (SIDE // 2, SIDE // 2, 8, C)
    early = lax.broadcasted_iota(jnp.int32, (SIDE // 2, 1, 8, C), 2) < 4
    left = pltpu.roll(values, 4, 0).reshape(tiles)
    left = jnp.concatenate([jnp.where(early, 0.0, left[:, :1]), left[:, 1:]], axis=1)
    right = pltpu.roll(values, ROWS - 4, 0).reshape(tiles)
    right = jnp.concatenate([right[:, :-1], jnp.where(early, right[:, -1:], 0.0)], axis=1)
    return left.reshape(ROWS, C), values, right.reshape(ROWS, C)


def bordered(values):
    even = even_pairs((LINE, C))
    above = jnp.where(even, 0.0, pltpu.roll(values[ROWS - LINE :], 2, 0))
    below = jnp.where(even, pltpu.roll(values[:LINE], LINE - 2, 0), 0.0)
    return jnp.concatenate([above, values, below], axis=0).astype(BF16)


def columns_of(sides):
    return jnp.concatenate(
        [side[kr * LINE : kr * LINE + ROWS] for kr in range(3) for side in sides], axis=1
    )


def kernel(
    order_ref,
    act_hbm,
    fresh_act_hbm,
    saved_hbm,
    grad_hbm,
    fresh_grad_hbm,
    fw_hbm,
    fgain_ref,
    fbias_ref,
    bw_hbm,
    bgain_ref,
    bbias_ref,
    emitted_hbm,
    returned_hbm,
    wgrad_ref,
    act_ref,
    fresh_act_ref,
    saved_ref,
    grad_ref,
    fresh_grad_ref,
    fw_ref,
    bw_ref,
    emitted_ref,
    returned_ref,
    x_buf,
    e_buf,
    xhat_buf,
    slope_buf,
    scale_buf,
    hidden_buf,
    turned_buf,
    bwt_buf,
    border_buf,
    total_buf,
    act_out,
    act_in,
    grad_out,
    grad_in,
    y_in,
    y_sum,
    z_in,
    z_mid,
    far_in,
    act_send,
    act_recv,
    grad_send,
    grad_recv,
    y_send,
    y_recv,
    z_send,
    z_recv,
    far_send,
    far_recv,
    load_sem,
    emitted_sem,
    returned_sem,
):
    section = lax.axis_index("section")
    shard = lax.axis_index("dp")
    my_y = shard // NZ
    my_z = lax.rem(shard, NZ)
    my_q = my_z // QUAD
    my_w = lax.rem(my_z, QUAD)

    barrier = pltpu.get_barrier_semaphore()
    for near in (lax.rem(section + 1, SECTIONS), lax.rem(section + SECTIONS - 1, SECTIONS)):
        pl.semaphore_signal(
            barrier, inc=1, device_id={"section": near, "dp": shard}, device_id_type=MESH
        )
    for k in range(1, NY):
        peer = lax.rem(my_y + k, NY) * NZ + my_z
        pl.semaphore_signal(
            barrier, inc=1, device_id={"section": section, "dp": peer}, device_id_type=MESH
        )
    far = lax.rem(my_z + QUAD, NZ)
    for peer in [my_q * QUAD + lax.rem(my_w + k, QUAD) for k in range(1, QUAD)] + [far]:
        pl.semaphore_signal(
            barrier,
            inc=1,
            device_id={"section": section, "dp": my_y * NZ + peer},
            device_id_type=MESH,
        )

    loads = [
        pltpu.make_async_copy(source, buf, load_sem.at[i])
        for i, (source, buf) in enumerate(
            (
                (bw_hbm, bw_ref),
                (saved_hbm, saved_ref),
                (grad_hbm, grad_ref),
                (fw_hbm, fw_ref),
                (act_hbm, act_ref),
                (fresh_grad_hbm, fresh_grad_ref),
                (fresh_act_hbm, fresh_act_ref),
            )
        )
    ]
    for load in loads:
        load.start()

    def sender(out, into, send, recv, tick):
        return pltpu.make_async_remote_copy(
            src_ref=out.at[tick],
            dst_ref=into.at[tick],
            send_sem=send.at[tick],
            recv_sem=recv.at[tick],
            device_id={"section": lax.rem(section + 1, SECTIONS), "dp": shard},
            device_id_type=MESH,
        )

    def send_on(*stream):
        @pl.when(section < SECTIONS - 1)
        def _():
            sender(*stream).start()

    def send_from(core, *stream):
        @pl.when(jnp.logical_and(section < SECTIONS - 1, lax.rem(section, 2) == core))
        def _():
            sender(*stream).start()

    def sent(*stream):
        @pl.when(section < SECTIONS - 1)
        def _():
            sender(*stream).wait_send()

    def take(buf, fresh_ref, stream, tick):
        @pl.when(section == 0)
        def _():
            buf[...] = worked(fresh_ref[order_ref[tick - 1]].astype(F32)).reshape(TILES, 8, C)

        @pl.when(section > 0)
        def _():
            sender(*stream).wait_recv()
            buf[...] = stream[1][tick - 1]

    act_stream = lambda tick: (act_out, act_in, act_send, act_recv, tick)
    grad_stream = lambda tick: (grad_out, grad_in, grad_send, grad_recv, tick)

    def prepare(tick):
        values = worked(saved_ref[tick].astype(F32)).reshape(TILES, 8, C)
        xhat, scale = normed(values)
        gain = bgain_ref[...]
        scaled = xhat * gain + bbias_ref[...]
        gate = 1.0 / (1.0 + jnp.exp(-scaled))
        xhat_buf[tick] = xhat
        scale_buf[tick] = scale
        slope_buf[tick] = gate * (1.0 + scaled * (1.0 - gate)) * gain
        hidden_buf[tick] = scaled * gate

    def turn(tick):
        for kc, side in enumerate(sideways(hidden_buf[tick].reshape(ROWS, C))):
            turned_buf[tick, kc * C : (kc + 1) * C] = side.T.astype(BF16)

    def backward(tick):
        incoming = e_buf[...]
        sides = [bordered(side) for side in sideways(incoming.reshape(ROWS, C))]
        border_buf[...] = sides[1]
        hidden_grad = jnp.dot(columns_of(sides), bwt_buf[...], preferred_element_type=F32)
        through = hidden_grad.reshape(TILES, 8, C) * slope_buf[tick]
        xhat = xhat_buf[tick]
        level = group_mean(through)
        tilt = group_mean(through * xhat)
        return incoming + scale_buf[tick] * (through - level - xhat * tilt)

    def weight_terms(tick):
        for kr in range(3):
            shifted = border_buf[(2 - kr) * LINE : (2 - kr) * LINE + ROWS]
            term = jnp.dot(turned_buf[tick], shifted, preferred_element_type=F32)
            rows = pl.ds(kr * 3 * C, 3 * C)
            if tick == 0:
                total_buf[rows] = term
            else:
                total_buf[rows] += term

    def forward():
        values = x_buf[...]
        xhat, _ = normed(values)
        scaled = xhat * fgain_ref[...] + fbias_ref[...]
        hidden = scaled / (1.0 + jnp.exp(-scaled))
        sides = [bordered(side) for side in sideways(hidden.reshape(ROWS, C))]
        mixed = jnp.dot(columns_of(sides), fw_ref[...], preferred_element_type=F32)
        return values + mixed.reshape(TILES, 8, C)

    def written(side, tick):
        buf, out, sem = side
        return pltpu.make_async_copy(buf.at[tick], out.at[tick], sem.at[tick])

    def store(side, tick, values):
        side[0][tick] = stored(values.reshape(ROWS, C))
        written(side, tick).start()

    emitted_side = (emitted_ref, emitted_hbm, emitted_sem)
    returned_side = (returned_ref, returned_hbm, returned_sem)

    loads[0].wait()
    for kr in range(3):
        for kc in range(3):
            mirrored = ((2 - kr) * 3 + 2 - kc) * C
            bwt_buf[(kr * 3 + kc) * C : (kr * 3 + kc + 1) * C] = bw_ref[mirrored : mirrored + C].T

    loads[1].wait()
    prepare(0)
    loads[2].wait()
    e_buf[...] = worked(grad_ref[...].astype(F32)).reshape(TILES, 8, C)
    grad_out[0] = backward(0)
    loads[3].wait()
    loads[4].wait()
    x_buf[...] = worked(act_ref[...].astype(F32)).reshape(TILES, 8, C)
    act_out[0] = forward()
    pl.semaphore_wait(barrier, 2 + NY - 1 + QUAD)
    send_on(*grad_stream(0))
    send_from(0, *act_stream(0))
    store(returned_side, 0, grad_out[0])
    store(emitted_side, 0, act_out[0])
    prepare(1)
    loads[5].wait()
    loads[6].wait()
    turn(0)
    weight_terms(0)

    take(e_buf, fresh_grad_ref, grad_stream(0), 1)
    grad_out[1] = backward(1)
    sent(*grad_stream(0))
    send_on(*grad_stream(1))
    store(returned_side, 1, grad_out[1])
    turn(1)
    weight_terms(1)
    for tick in (2, 3):
        prepare(tick)
        turn(tick)
    take(e_buf, fresh_grad_ref, grad_stream(1), 2)
    grad_out[2] = backward(2)
    sent(*grad_stream(1))
    send_on(*grad_stream(2))
    store(returned_side, 2, grad_out[2])
    weight_terms(2)

    take(e_buf, fresh_grad_ref, grad_stream(2), 3)
    store(returned_side, 3, backward(3))
    weight_terms(3)

    total = total_buf.reshape(NY, NZ, BLOCK, C)

    def y_copy(part, k):
        peer = lax.rem(my_y + k, NY)
        return pltpu.make_async_remote_copy(
            src_ref=total.at[peer, :, pl.ds(part * PIECE, PIECE)],
            dst_ref=y_in.at[part, NY - 1 - k],
            send_sem=y_send.at[part, k - 1],
            recv_sem=y_recv.at[part, NY - 1 - k],
            device_id={"section": section, "dp": peer * NZ + my_z},
            device_id_type=MESH,
        )

    def z_copy(part, k):
        peer = lax.rem(my_w + k, QUAD)
        return pltpu.make_async_remote_copy(
            src_ref=y_sum.at[part, :, peer],
            dst_ref=z_in.at[part, QUAD - 1 - k],
            send_sem=z_send.at[part, k - 1],
            recv_sem=z_recv.at[part, QUAD - 1 - k],
            device_id={"section": section, "dp": my_y * NZ + my_q * QUAD + peer},
            device_id_type=MESH,
        )

    def far_copy(part):
        return pltpu.make_async_remote_copy(
            src_ref=z_mid.at[part, 1 - my_q],
            dst_ref=far_in.at[part],
            send_sem=far_send.at[part],
            recv_sem=far_recv.at[part],
            device_id={"section": section, "dp": my_y * NZ + far},
            device_id_type=MESH,
        )

    def y_done(part):
        for k in range(1, NY):
            y_copy(part, k).wait_recv()
        piece = total[my_y, :, pl.ds(part * PIECE, PIECE)] + (
            y_in[part, 0] + y_in[part, 1] + y_in[part, 2]
        )
        y_sum[part] = piece.reshape(NZ // QUAD, QUAD, PIECE, C)
        for k in (2, 1, 3):
            z_copy(part, k).start()

    def y_start(part):
        for k in (2, 1, 3):
            y_copy(part, k).start()

    def y_sent(part):
        for k in range(1, NY):
            y_copy(part, k).wait_send()

    y_start(0)
    y_start(1)
    sent(*grad_stream(2))
    send_from(1, *act_stream(0))
    take(x_buf, fresh_act_ref, act_stream(0), 1)
    act_out[1] = forward()
    send_from(0, *act_stream(1))
    store(emitted_side, 1, act_out[1])
    y_sent(0)
    y_done(0)
    sent(*act_stream(0))
    send_from(1, *act_stream(1))
    y_sent(1)
    y_start(2)
    y_done(1)
    take(x_buf, fresh_act_ref, act_stream(1), 2)
    act_out[2] = forward()
    sent(*act_stream(1))
    send_on(*act_stream(2))
    store(emitted_side, 2, act_out[2])
    y_done(2)
    for part in range(PARTS):
        for k in range(1, QUAD):
            z_copy(part, k).wait_recv()
        z_mid[part] = y_sum[part, :, my_w] + (z_in[part, 0] + z_in[part, 1] + z_in[part, 2])
        far_copy(part).start()

    take(x_buf, fresh_act_ref, act_stream(2), 3)
    store(emitted_side, 3, forward())

    for part in range(PARTS):
        far_copy(part).wait_recv()
        block = z_mid[part, my_q] + far_in[part]
        wgrad_ref[part * PIECE : (part + 1) * PIECE] = block * (1.0 / BATCH)

    sent(*act_stream(2))

    y_sent(PARTS - 1)
    for part in range(PARTS):
        for k in range(1, QUAD):
            z_copy(part, k).wait_send()
        far_copy(part).wait_send()

    for tick in range(TICKS):
        written(emitted_side, tick).wait()
        written(returned_side, tick).wait()


def as_rows(images):
    lead = images.shape[:-4]
    n = len(lead)
    split = images.reshape(lead + (IMAGES, SIDE, SIDE, 2, HALF))
    turned = split.transpose(tuple(range(n)) + (n + 1, n + 2, n + 3, n, n + 4))
    return turned.reshape(lead + (NATIVE, HALF))


def as_images(rows):
    lead = rows.shape[:-2]
    n = len(lead)
    split = rows.reshape(lead + (SIDE, SIDE, 2, IMAGES, HALF))
    turned = split.transpose(tuple(range(n)) + (n + 3, n, n + 1, n + 2, n + 4))
    return turned.reshape(lead + (IMAGES, SIDE, SIDE, C))


def shards(
    arriving_activations,
    fresh_images,
    saved_inputs,
    arriving_gradients,
    fresh_gradients,
    feed_order,
    forward_weight,
    forward_gain,
    forward_bias,
    backward_weight,
    backward_gain,
    backward_bias,
):
    vmem = pl.BlockSpec(memory_space=pltpu.VMEM)
    whole = pl.BlockSpec(memory_space=pl.ANY)
    dma = pltpu.SemaphoreType.DMA
    tile = (TILES, 8, C)
    relay = pltpu.VMEM((TICKS - 1,) + tile, F32)
    emitted, returned, block = pl.pallas_call(
        kernel,
        out_shape=(
            jax.ShapeDtypeStruct((TICKS, NATIVE, HALF), F32),
            jax.ShapeDtypeStruct((TICKS, NATIVE, HALF), F32),
            jax.ShapeDtypeStruct((BLOCK, C), F32),
        ),
        in_specs=[pl.BlockSpec(memory_space=pltpu.SMEM)]
        + [whole] * 6
        + [vmem] * 2
        + [whole]
        + [vmem] * 2,
        out_specs=(whole, whole, vmem),
        scratch_shapes=[
            pltpu.VMEM((NATIVE, HALF), BF16),
            pltpu.VMEM((TICKS - 1, NATIVE, HALF), BF16),
            pltpu.VMEM((TICKS, NATIVE, HALF), BF16),
            pltpu.VMEM((NATIVE, HALF), BF16),
            pltpu.VMEM((TICKS - 1, NATIVE, HALF), BF16),
            pltpu.VMEM((TAPS * C, C), BF16),
            pltpu.VMEM((TAPS * C, C), BF16),
            pltpu.VMEM((TICKS, NATIVE, HALF), F32),
            pltpu.VMEM((TICKS, NATIVE, HALF), F32),
            pltpu.VMEM(tile, F32),
            pltpu.VMEM(tile, F32),
            pltpu.VMEM((TICKS,) + tile, F32),
            pltpu.VMEM((TICKS,) + tile, F32),
            pltpu.VMEM((TICKS, 8, C), F32),
            pltpu.VMEM((TICKS,) + tile, F32),
            pltpu.VMEM((TICKS, 3 * C, ROWS), BF16),
            pltpu.VMEM((TAPS * C, C), BF16),
            pltpu.VMEM((ROWS + 2 * LINE, C), BF16),
            pltpu.VMEM((TAPS * C, C), F32),
            relay,
            relay,
            relay,
            relay,
            pltpu.VMEM((PARTS, NY - 1, NZ, PIECE, C), F32),
            pltpu.VMEM((PARTS, NZ // QUAD, QUAD, PIECE, C), F32),
            pltpu.VMEM((PARTS, QUAD - 1, NZ // QUAD, PIECE, C), F32),
            pltpu.VMEM((PARTS, NZ // QUAD, PIECE, C), F32),
            pltpu.VMEM((PARTS, PIECE, C), F32),
            dma((TICKS - 1,)),
            dma((TICKS - 1,)),
            dma((TICKS - 1,)),
            dma((TICKS - 1,)),
            dma((PARTS, NY - 1)),
            dma((PARTS, NY - 1)),
            dma((PARTS, QUAD - 1)),
            dma((PARTS, QUAD - 1)),
            dma((PARTS,)),
            dma((PARTS,)),
            dma((7,)),
            dma((TICKS,)),
            dma((TICKS,)),
        ],
        compiler_params=pltpu.CompilerParams(
            collective_id=0, has_side_effects=True, vmem_limit_bytes=60 * 1024 * 1024
        ),
    )(
        feed_order,
        as_rows(arriving_activations[0]),
        as_rows(fresh_images),
        as_rows(saved_inputs[:, 0]),
        as_rows(arriving_gradients[0]),
        as_rows(fresh_gradients),
        forward_weight[0],
        forward_gain,
        forward_bias,
        backward_weight[0],
        backward_gain,
        backward_bias,
    )
    return (as_images(emitted)[:, None], as_images(returned)[:, None], block[None])


def solution(mesh):
    placed = (
        P("section", "dp", None, None, None),
        P(None, "dp", None, None, None),
        P(None, "section", "dp", None, None, None),
        P("section", "dp", None, None, None),
        P(None, "dp", None, None, None),
        P(),
        P("section", None, None),
        P("section", None),
        P("section", None),
        P("section", None, None),
        P("section", None),
        P("section", None),
    )
    return jax.shard_map(
        shards,
        mesh=mesh,
        in_specs=placed,
        out_specs=(
            P(None, "section", "dp", None, None, None),
            P(None, "section", "dp", None, None, None),
            P("section", "dp", None),
        ),
        check_vma=False,
    )
```
